1024 devices in a mesh: ctx: 128 (over y, z, core), head: 8 (over x).
Axes of the slice: x: 8, y: 8, z: 8, core: 2. Of those that a mesh axis runs over, the one named last changes fastest.
Arguments:
- query: bfloat16 [16384, 4096], P('ctx', 'head'), may hold values from -6 to 6
- keys: bfloat16 [16384, 4096], P('ctx', 'head'), may hold values from -10 to 10
- values: bfloat16 [16384, 4096], P('ctx', 'head'), may hold values from -12 to 12
- log_decay: float32 [16384, 32], P('ctx', 'head'), may hold values from -1 to 0
- norm_gain: float32 [4096], P('head'), may hold values from 0.1 to 1.9
- out_weight: bfloat16 [4096, 6144], P('head'), may hold values from -0.125 to 0.125
Outputs:
- mixed: bfloat16 [16384, 6144], P('ctx', 'head')
The draws below stay inside these ranges and needn't reach their ends.
All inputs are finite; a program needn't handle non-finite values.
Results may differ from the reference program's by a relative error of at most 0.014.
Values may be sent and summed in bfloat16 or wider, within the bound.
A program may use at most 128 MiB of HBM per device.

```python
import jax
import jax.numpy as jnp
from jax import lax

D = 6144
DH = 128
TOK_DEV = 128
HEAD_TOTAL = 32
PROMPT_TOKENS = 16384
N_HEAD = 8


def slab_levels(level_key, lower_end, upper_end):
    block_count = PROMPT_TOKENS // TOK_DEV
    raw_level = jax.random.uniform(level_key, (block_count, HEAD_TOTAL), jnp.float32, lower_end, upper_end)
    spread = jnp.repeat(jnp.exp(raw_level), TOK_DEV, axis=0)
    return jnp.repeat(spread, DH, axis=1)


def draw_keys(key, part):
    key_sequence = jax.random.split(jax.random.fold_in(key, 11), 2)
    entries = jnp.clip(jax.random.normal(key_sequence[0], (PROMPT_TOKENS, HEAD_TOTAL * DH), jnp.float32), -3.5, 3.5)
    return (entries * slab_levels(key_sequence[1], -1.2, 1.0)).astype(jnp.bfloat16)


def draw_values(key, part):
    key_sequence = jax.random.split(jax.random.fold_in(key, 23), 2)
    entries = jnp.clip(jax.random.normal(key_sequence[0], (PROMPT_TOKENS, HEAD_TOTAL * DH), jnp.float32), -3.5, 3.5)
    return (entries * slab_levels(key_sequence[1], -1.5, 1.2)).astype(jnp.bfloat16)


def draw_log_decay(key, part):
    key_sequence = jax.random.split(jax.random.fold_in(key, 5), 6)
    fast_share = 0.5
    is_fast = jax.random.uniform(key_sequence[0], (HEAD_TOTAL,)) < fast_share
    fast_rate = jnp.exp(jax.random.uniform(key_sequence[1], (HEAD_TOTAL,), jnp.float32, jnp.log(1.0 / (2.0 * TOK_DEV + 40.0)), jnp.log(1.0 / 30.0)))
    slow_rate = jnp.exp(jax.random.uniform(key_sequence[2], (HEAD_TOTAL,), jnp.float32, jnp.log(0.05), jnp.log(0.4))) / PROMPT_TOKENS
    base_rate = jnp.where(is_fast, fast_rate, slow_rate)
    block_count = PROMPT_TOKENS // TOK_DEV
    factor = jnp.exp(jax.random.uniform(key_sequence[3], (block_count, HEAD_TOTAL), jnp.float32, jnp.log(0.7), jnp.log(2.8)))
    decay_rate_lookup = jnp.repeat(factor, TOK_DEV, axis=0) * base_rate[None, :]
    spike_positions = jax.random.randint(key_sequence[4], (2, HEAD_TOTAL), 0, PROMPT_TOKENS)
    token_offset = jnp.arange(PROMPT_TOKENS)[:, None]
    spike_present = ((token_offset == spike_positions[0][None, :]) | (token_offset == spike_positions[1][None, :])).astype(jnp.float32)
    spike_penalty = jax.random.uniform(key_sequence[5], (PROMPT_TOKENS, HEAD_TOTAL), jnp.float32, 0.2, 0.4)
    return -(decay_rate_lookup - spike_present * jnp.log(1.0 - spike_penalty))


def raised(values, stream_key, source, target, parts, factor):
    owner, partner = [(jnp.arange(values.shape[dim]) // (values.shape[dim] // parts)).reshape([-1 if axis == dim else 1 for axis in range(values.ndim)]) for dim in (source, target)]
    chosen = jax.random.permutation(stream_key, parts)[partner]
    strong = (owner == chosen) | (owner == (partner + parts // 2) % parts)
    return jnp.where(strong, factor * values, values)


def block_levels(rng, extent, cuts, low, largest):
    factor_of, own = 1.0, jax.random.fold_in(rng, 6)
    for position, blocks in cuts:
        draws = jnp.exp(jax.random.uniform(jax.random.fold_in(own, position), (blocks,), jnp.float32, low / len(cuts), largest / len(cuts)))
        factor_of = factor_of * jnp.repeat(draws, extent[position] // blocks).reshape([-1 if axis == position else 1 for axis in range(len(extent))])
    return factor_of


def gaussian(rng, dims, width, reach, pieces=(), held_as=jnp.bfloat16):
    loudness = block_levels(rng, dims, pieces, -0.22, 0.18) if pieces else 1.0
    drawn = jax.random.normal(rng, dims, jnp.float32) * width * loudness
    return jnp.minimum(jnp.maximum(drawn, -reach), reach).astype(held_as)


def noise_with(key, extent, scale, limit, cuts, heavy, kind=jnp.bfloat16):
    drawn = scale * jax.random.normal(key, extent, jnp.float32)
    if cuts:
        drawn = drawn * block_levels(key, extent, cuts, -0.22, 0.18)
    return jnp.clip(raised(drawn, jax.random.fold_in(key, 3), *heavy), -limit, limit).astype(kind)


def setup_inputs(seed: int = 0) -> dict:
    streams_of = jax.random.split(jax.random.key(seed), 7)
    return {
        "query": gaussian(streams_of[0], (PROMPT_TOKENS, HEAD_TOTAL * DH), 1.0, 6.0, ((0, 128), (1, 8))),
        "keys": draw_keys(jax.random.fold_in(streams_of[6], 71), 0),
        "values": draw_values(jax.random.fold_in(streams_of[6], 71), 0),
        "log_decay": draw_log_decay(jax.random.fold_in(streams_of[6], 71), 0),
        "norm_gain": jnp.clip(1.0 + 0.18 * jax.random.normal(streams_of[4], (HEAD_TOTAL * DH,), jnp.float32), 0.1, 1.9),
        "out_weight": noise_with(streams_of[5], (HEAD_TOTAL * DH, D), (HEAD_TOTAL * DH) ** -0.5, 0.125, ((0, 8),), (0, 1, 8, 2.0)),
    }


def reference(query, keys, values, log_decay, norm_gain, out_weight):
    head_count = log_decay.shape[1]
    full_width = query.shape[1]
    head_dim = full_width // head_count
    block_count = query.shape[0] // TOK_DEV

    def to_blocks(array):
        return array.reshape(block_count, TOK_DEV, head_count, head_dim).transpose(0, 2, 1, 3)
    query_blocks = to_blocks(query)
    key_blocks = to_blocks(keys)
    value_blocks = to_blocks(values)
    decay_blocks = log_decay.reshape(block_count, TOK_DEV, head_count).transpose(0, 2, 1)
    row_index = lax.broadcasted_iota(jnp.int32, (TOK_DEV, TOK_DEV), 0)
    col_index = lax.broadcasted_iota(jnp.int32, (TOK_DEV, TOK_DEV), 1)
    causal = (row_index >= col_index)[None]

    def step(state, item):
        queries, key_rows, value_rows, decay = item
        cumulative = jnp.cumsum(decay, axis=1)
        differ = jnp.where(causal, cumulative[:, :, None] - cumulative[:, None, :], -1e+30)
        scores = jnp.einsum('hte,hse->hts', queries.astype(jnp.float32), key_rows.astype(jnp.float32))
        block_weights = (jnp.exp(differ) * scores).astype(jnp.bfloat16)
        within = jnp.einsum('hts,hse->hte', block_weights.astype(jnp.float32), value_rows.astype(jnp.float32))
        carried_part = jnp.exp(cumulative)[:, :, None] * jnp.einsum('hte,hef->htf', queries.astype(jnp.float32), state, precision=lax.Precision.HIGHEST)
        tail_decay = jnp.exp(cumulative[:, -1:] - cumulative)
        kv_local = jnp.einsum('hte,htf->hef', key_rows.astype(jnp.float32) * tail_decay[:, :, None], value_rows.astype(jnp.float32), precision=lax.Precision.HIGHEST)
        new_state = jnp.exp(cumulative[:, -1])[:, None, None] * state + kv_local
        return (new_state, within + carried_part)
    start_state = jnp.zeros((head_count, head_dim, head_dim), jnp.float32)
    _, outputs = lax.scan(step, start_state, (query_blocks, key_blocks, value_blocks, decay_blocks))
    attn = outputs.transpose(0, 2, 1, 3).reshape(query.shape[0], full_width)
    mean_square = lax.optimization_barrier(jnp.mean(attn * attn, axis=1))
    normed = (attn * lax.rsqrt(mean_square + 1e-05)[:, None] * norm_gain[None, :]).astype(jnp.bfloat16)
    group_width = full_width // N_HEAD
    summed = jnp.zeros((query.shape[0], out_weight.shape[1]), jnp.float32)
    for group in range(N_HEAD):
        piece = jnp.dot(normed[:, group * group_width:(group + 1) * group_width], out_weight[group * group_width:(group + 1) * group_width], preferred_element_type=jnp.float32)
        summed = summed + lax.optimization_barrier(piece.astype(jnp.bfloat16)).astype(jnp.float32)
    return summed.astype(jnp.bfloat16)
```

```python
import functools

import jax
import jax.numpy as jnp
from jax import lax
from jax.experimental import pallas as pl
from jax.experimental.pallas import tpu as pltpu
from jax.sharding import PartitionSpec as P

MESH = pl.DeviceIdType.MESH
HIGHEST = lax.Precision.HIGHEST
LANE = 128
ROW_GROUP = 16
F32 = jnp.float32
BF16 = jnp.bfloat16


def body(
    dims,
    q_hbm, k_hbm, v_hbm, ld_hbm, gain_hbm, w_hbm,
    out_ref,
    q, k, v, ld, gain, w,
    cc, within, act,
    d_send, d_recv, s_send, z_recv, e_buf, pd_buf,
    yd_send, yd_recv, r_send, y_recv, p_send, s_in,
    sq_send, sq_recv, own, tx, rx,
    in_sem, w_sem, d_sem, z_sem, yd_sem, y_send_sem, y_recv_sem, p_sem, sq_sem,
    tx_sem, rx_sem,
):
    nx, ny, group, heads, chunks = dims
    x = lax.axis_index("head")
    ctx = lax.axis_index("ctx")
    y = ctx // group
    j = lax.rem(ctx, group)
    base = y * group
    rows = s_send.shape[1]
    half_x = nx // 2
    half_c = chunks // 2
    width = chunks * LANE
    per_head = LANE // rows

    barrier = pltpu.get_barrier_semaphore()

    def greet_row(r, _):
        pl.semaphore_signal(
            barrier, inc=1, device_id={"ctx": base + lax.rem(j + r, group)}, device_id_type=MESH
        )
        return 0

    def greet_y(r, _):
        pl.semaphore_signal(
            barrier, inc=1, device_id={"ctx": lax.rem(y + r, ny) * group + j}, device_id_type=MESH
        )
        return 0

    def greet_x(r, _):
        pl.semaphore_signal(
            barrier, inc=1, device_id={"head": lax.rem(x + r, nx)}, device_id_type=MESH
        )
        return 0

    ld_in = pltpu.make_async_copy(ld_hbm, ld, in_sem.at[0])
    k_in = pltpu.make_async_copy(k_hbm, k, in_sem.at[1])
    v_in = pltpu.make_async_copy(v_hbm, v, in_sem.at[2])
    q_in = pltpu.make_async_copy(q_hbm, q, in_sem.at[3])
    gain_in = pltpu.make_async_copy(gain_hbm, gain, in_sem.at[4])
    for copy in (ld_in, k_in, v_in, q_in, gain_in):
        copy.start()
    lax.fori_loop(1, group, greet_row, 0)
    lax.fori_loop(1, ny, greet_y, 0)
    lax.fori_loop(1, nx, greet_x, 0)

    row_index = lax.broadcasted_iota(jnp.int32, (LANE, LANE), 0)
    col_index = lax.broadcasted_iota(jnp.int32, (LANE, LANE), 1)
    upper = jnp.where(row_index <= col_index, 1.0, 0.0).astype(F32)
    ld_in.wait()
    cum = jnp.dot(ld[...], upper, precision=HIGHEST, preferred_element_type=F32)
    for h in range(heads):
        spread = jnp.transpose(jnp.broadcast_to(cum[h : h + 1, :], (LANE, LANE)))
        cc[h] = spread
        d_send[h] = jnp.exp(spread[LANE - 1 : LANE, :])

    pl.semaphore_wait(barrier, (group - 1) + (ny - 1) + (nx - 1))

    def send_decay(r, _):
        owner = lax.rem(j + r, group)
        pltpu.make_async_remote_copy(
            src_ref=d_send.at[owner // per_head],
            dst_ref=d_recv.at[j],
            send_sem=d_sem.at[0],
            recv_sem=d_sem.at[1],
            device_id={"ctx": base + owner},
            device_id_type=MESH,
        ).start()
        return 0

    lax.fori_loop(1, group, send_decay, 0)
    d_recv[pl.ds(j, 1)] = d_send[pl.ds(j // per_head, 1)]

    k_in.wait()
    v_in.wait()
    for h in range(heads):
        columns = slice(h * LANE, (h + 1) * LANE)
        spread = cc[h]
        tail = jnp.exp(spread[LANE - 1 : LANE, :] - spread)
        faded = (k[:, columns].astype(F32) * tail).astype(BF16)
        state = lax.dot_general(
            faded, v[:, columns], (((0,), (0,)), ((), ())), preferred_element_type=F32
        )
        s_send[h * per_head : (h + 1) * per_head] = state.astype(BF16).reshape(per_head, rows, LANE)

        def send_slice(owner, _):
            @pl.when(owner != j)
            def _():
                pltpu.make_async_remote_copy(
                    src_ref=s_send.at[owner],
                    dst_ref=z_recv.at[j],
                    send_sem=z_sem.at[0],
                    recv_sem=z_sem.at[1],
                    device_id={"ctx": base + owner},
                    device_id_type=MESH,
                ).start()

            return 0

        lax.fori_loop(h * per_head, (h + 1) * per_head, send_slice, 0)
    z_recv[pl.ds(j, 1)] = s_send[pl.ds(j, 1)]

    def weight_copy(r):
        start = pl.multiple_of(lax.rem(x + r, nx) * width, LANE)
        return pltpu.make_async_copy(w_hbm.at[:, pl.ds(start, width)], w.at[r], w_sem.at[r])

    for step in range(half_x):
        distance = half_x - step
        for r in sorted({distance, nx - distance}):
            weight_copy(r).start()
    weight_copy(0).start()

    def bulk(ref, send_sem, recv_sem):
        return pltpu.make_async_remote_copy(
            src_ref=ref, dst_ref=ref, send_sem=send_sem, recv_sem=recv_sem,
            device_id={"head": lax.rem(x + 1, nx)}, device_id_type=MESH,
        )

    bulk(d_recv.at[pl.ds(0, group - 1)], d_sem.at[0], d_sem.at[1]).wait_recv()
    running = jnp.ones((1, LANE), F32)
    for i in range(group):
        pd_buf[i] = running
        running = running * d_recv[i]
    yd_send[0] = running

    def send_row_decay(r, _):
        pltpu.make_async_remote_copy(
            src_ref=yd_send.at[0],
            dst_ref=yd_recv.at[y],
            send_sem=yd_sem.at[0],
            recv_sem=yd_sem.at[1],
            device_id={"ctx": lax.rem(y + r, ny) * group + j},
            device_id_type=MESH,
        ).start()
        return 0

    if ny > 1:
        lax.fori_loop(1, ny, send_row_decay, 0)

    q_in.wait()
    causal = row_index >= col_index
    for h in range(heads):
        columns = slice(h * LANE, (h + 1) * LANE)
        spread = cc[h]
        scores = lax.dot_general(
            q[:, columns], k[:, columns], (((1,), (1,)), ((), ())), preferred_element_type=F32
        )
        differ = jnp.where(causal, spread - cum[h : h + 1, :], -1e30)
        weights = (jnp.exp(differ) * scores).astype(BF16)
        within[h] = jnp.dot(weights, v[:, columns], preferred_element_type=F32)
        cc[h] = jnp.exp(spread)

    bulk(z_recv.at[pl.ds(0, group - 1)], z_sem.at[0], z_sem.at[1]).wait_recv()
    carry = jnp.zeros((rows, LANE), F32)
    for i in range(group):
        e_buf[i] = carry
        carry = d_recv[i] * carry + z_recv[i].astype(F32)
    r_send[0] = carry.astype(BF16)

    def row_total(target):
        return pltpu.make_async_remote_copy(
            src_ref=r_send.at[0],
            dst_ref=y_recv.at[y],
            send_sem=y_send_sem.at[target],
            recv_sem=y_recv_sem.at[y],
            device_id={"ctx": target * group + j},
            device_id_type=MESH,
        )

    def send_total(target, _):
        row_total(target).start()
        return 0

    lax.fori_loop(y + 1, ny, send_total, 0)
    if ny > 1:
        bulk(yd_recv.at[pl.ds(0, ny - 1)], yd_sem.at[0], yd_sem.at[1]).wait_recv()

    def add_row(i, prefix):
        pltpu.make_async_remote_copy(
            src_ref=y_recv.at[i],
            dst_ref=y_recv.at[i],
            send_sem=y_send_sem.at[i],
            recv_sem=y_recv_sem.at[i],
            device_id={"ctx": i * group + j},
            device_id_type=MESH,
        ).wait_recv()
        return yd_recv[i] * prefix + y_recv[i].astype(F32)

    prefix = lax.fori_loop(0, y, add_row, jnp.zeros((rows, LANE), F32))

    def send_prefix(i, _):
        p_send[i] = (pd_buf[i] * prefix + e_buf[i]).astype(BF16)

        @pl.when(i != j)
        def _():
            pltpu.make_async_remote_copy(
                src_ref=p_send.at[i],
                dst_ref=s_in.at[j],
                send_sem=p_sem.at[0],
                recv_sem=p_sem.at[1],
                device_id={"ctx": base + i},
                device_id_type=MESH,
            ).start()

        return 0

    lax.fori_loop(0, group, send_prefix, 0)
    s_in[pl.ds(j, 1)] = p_send[pl.ds(j, 1)]

    gain_in.wait()
    for step in range(half_x):
        distance = half_x - step
        for r in sorted({distance, nx - distance}):
            weight_copy(r).wait()
    weight_copy(0).wait()

    bulk(s_in.at[pl.ds(0, group - 1)], p_sem.at[0], p_sem.at[1]).wait_recv()
    squares = jnp.zeros((LANE, LANE), F32)
    for h in range(heads):
        columns = slice(h * LANE, (h + 1) * LANE)
        state = s_in[h * per_head : (h + 1) * per_head].reshape(LANE, LANE)
        carried = jnp.dot(q[:, columns], state, preferred_element_type=F32)
        attn = within[h] + cc[h] * carried
        squares = squares + attn * attn
        act[:, columns] = (attn * gain[:, columns]).astype(BF16)

    right, left = lax.rem(x + 1, nx), lax.rem(x + nx - 1, nx)

    def slot(step, c, way):
        if step == 0:
            return c if way == 0 else c - half_c
        return half_c + chunks * (step - 1) + c

    def hop(step, c, way):
        place = slot(step, c, way)
        return pltpu.make_async_remote_copy(
            src_ref=tx.at[way, place],
            dst_ref=rx.at[way, place],
            send_sem=tx_sem.at[way],
            recv_sem=rx_sem.at[way, place],
            device_id={"head": right if way == 0 else left},
            device_id_type=MESH,
        )

    def project(r, pair):
        return jnp.dot(
            act[...], w[r, :, pair * 2 * LANE : (pair + 1) * 2 * LANE], preferred_element_type=F32
        )

    for pair in range(chunks // 2):
        block = project(half_x, pair)
        for c in (2 * pair, 2 * pair + 1):
            way = 0 if c < half_c else 1
            part = block[:, :LANE] if c % 2 == 0 else block[:, LANE:]
            tx[way, slot(0, c, way)] = part.astype(BF16)
            hop(0, c, way).start()

    sq_send[0] = jnp.sum(jnp.transpose(squares), axis=0, keepdims=True)

    def send_squares(r, _):
        pltpu.make_async_remote_copy(
            src_ref=sq_send.at[0],
            dst_ref=sq_recv.at[x],
            send_sem=sq_sem.at[0],
            recv_sem=sq_sem.at[1],
            device_id={"head": lax.rem(x + r, nx)},
            device_id_type=MESH,
        ).start()
        return 0

    lax.fori_loop(1, nx, send_squares, 0)
    sq_recv[pl.ds(x, 1)] = sq_send[...]

    def arrives(step, c, way):
        if step == 0:
            return (c < half_c) == (way == 0)
        return True

    def fill(way, r):
        for pair in range(chunks // 2):
            block = project(r, pair)
            own[way, 2 * pair] = block[:, :LANE]
            own[way, 2 * pair + 1] = block[:, LANE:]

    for step in range(1, half_x):
        distance = half_x - step
        fill(0, distance)
        fill(1, nx - distance)
        order = [list(range(chunks)), list(range(chunks))]
        if step == 1:
            order[0] = order[0][half_c:] + order[0][:half_c]
        for place in range(chunks):
            for way in (0, 1):
                c = order[way][place]
                total = own[way, c]
                if arrives(step - 1, c, way):
                    hop(step - 1, c, way).wait_recv()
                    total = total + rx[way, slot(step - 1, c, way)].astype(F32)
                tx[way, slot(step, c, way)] = total.astype(BF16)
                hop(step, c, way).start()

    fill(0, 0)
    bulk(sq_recv.at[pl.ds(0, nx - 1)], sq_sem.at[0], sq_sem.at[1]).wait_recv()
    total = sq_recv[0]
    for i in range(1, nx):
        total = total + sq_recv[i]
    scale = lax.rsqrt(total / (nx * heads * LANE) + 1e-05)
    scale = jnp.transpose(jnp.broadcast_to(scale, (LANE, LANE)))
    for c in range(chunks):
        block = own[0, c]
        for way in (0, 1):
            if arrives(half_x - 1, c, way):
                hop(half_x - 1, c, way).wait_recv()
                block = block + rx[way, slot(half_x - 1, c, way)].astype(F32)
        out_ref[:, c * LANE : (c + 1) * LANE] = (block * scale).astype(BF16)

    bulk(d_recv.at[pl.ds(0, group - 1)], d_sem.at[0], d_sem.at[1]).wait_send()
    bulk(z_recv.at[pl.ds(0, group - 1)], z_sem.at[0], z_sem.at[1]).wait_send()
    if ny > 1:
        bulk(yd_recv.at[pl.ds(0, ny - 1)], yd_sem.at[0], yd_sem.at[1]).wait_send()
    bulk(s_in.at[pl.ds(0, group - 1)], p_sem.at[0], p_sem.at[1]).wait_send()
    bulk(sq_recv.at[pl.ds(0, nx - 1)], sq_sem.at[0], sq_sem.at[1]).wait_send()

    def left_total(target, _):
        row_total(target).wait_send()
        return 0

    lax.fori_loop(y + 1, ny, left_total, 0)
    for way in (0, 1):
        bulk(tx.at[way], tx_sem.at[way], rx_sem.at[way, 0]).wait_send()


def solution(mesh, group=ROW_GROUP):
    nx, ctx = mesh.shape["head"], mesh.shape["ctx"]
    ny = ctx // group

    def local(query, keys, values, log_decay, norm_gain, out_weight):
        tokens, features = query.shape
        heads = log_decay.shape[1]
        width = out_weight.shape[1] // nx
        chunks = width // LANE
        rows = features // group
        slots = chunks // 2 + chunks * (nx // 2 - 1)
        anywhere = pl.BlockSpec(memory_space=pl.ANY)
        square = (LANE, LANE)
        dma = pltpu.SemaphoreType.DMA
        return pl.pallas_call(
            functools.partial(body, (nx, ny, group, heads, chunks)),
            out_shape=jax.ShapeDtypeStruct((tokens, width), BF16),
            in_specs=[anywhere] * 6,
            out_specs=pl.BlockSpec(memory_space=pltpu.VMEM),
            scratch_shapes=[
                pltpu.VMEM((tokens, features), BF16),
                pltpu.VMEM((tokens, features), BF16),
                pltpu.VMEM((tokens, features), BF16),
                pltpu.VMEM((heads, tokens), F32),
                pltpu.VMEM((1, features), F32),
                pltpu.VMEM((nx, features, width), BF16),
                pltpu.VMEM((heads,) + square, F32),
                pltpu.VMEM((heads,) + square, F32),
                pltpu.VMEM((tokens, features), BF16),
                pltpu.VMEM((heads, 1, LANE), F32),
                pltpu.VMEM((group, 1, LANE), F32),
                pltpu.VMEM((group, rows, LANE), BF16),
                pltpu.VMEM((group, rows, LANE), BF16),
                pltpu.VMEM((group, rows, LANE), F32),
                pltpu.VMEM((group, 1, LANE), F32),
                pltpu.VMEM((1, 1, LANE), F32),
                pltpu.VMEM((ny, 1, LANE), F32),
                pltpu.VMEM((1, rows, LANE), BF16),
                pltpu.VMEM((ny, rows, LANE), BF16),
                pltpu.VMEM((group, rows, LANE), BF16),
                pltpu.VMEM((group, rows, LANE), BF16),
                pltpu.VMEM((1, 1, LANE), F32),
                pltpu.VMEM((nx, 1, LANE), F32),
                pltpu.VMEM((2, chunks) + square, F32),
                pltpu.VMEM((2, slots) + square, BF16),
                pltpu.VMEM((2, slots) + square, BF16),
                dma((5,)),
                dma((nx,)),
                dma((2,)),
                dma((2,)),
                dma((2,)),
                dma((ny,)),
                dma((ny,)),
                dma((2,)),
                dma((2,)),
                dma((2,)),
                dma((2, slots)),
            ],
            compiler_params=pltpu.CompilerParams(
                collective_id=0, has_side_effects=True, vmem_limit_bytes=60 * 2**20
            ),
        )(query, keys, values, log_decay.T, norm_gain.reshape(1, features), out_weight)

    placed = (
        P("ctx", "head"),
        P("ctx", "head"),
        P("ctx", "head"),
        P("ctx", "head"),
        P("head"),
        P("head", None),
    )
    return jax.shard_map(
        local, mesh=mesh, in_specs=placed, out_specs=P("ctx", "head"), check_vma=False
    )
```

```python
import functools

import jax
import jax.numpy as jnp
from jax import lax
from jax.experimental import pallas as pl
from jax.experimental.pallas import tpu as pltpu
from jax.sharding import PartitionSpec as P

MESH = pl.DeviceIdType.MESH
HIGHEST = lax.Precision.HIGHEST
LANE = 128
ROW_GROUP = 16
F32 = jnp.float32
BF16 = jnp.bfloat16


def body(
    dims,
    q_hbm, k_hbm, v_hbm, ld_hbm, gain_hbm, w_hbm,
    out_ref,
    q, k, v, ld, gain, w,
    cc, within, act,
    d_send, d_recv, s_send, z_recv, e_buf, pd_buf,
    yd_send, yd_recv, r_send, y_recv, p_send, s_in,
    sq_send, sq_recv, own, tx, rx,
    in_sem, w_sem, d_sem, z_sem, yd_sem, y_send_sem, y_recv_sem, p_sem, sq_sem,
    tx_sem, rx_sem,
):
    nx, ny, group, heads, chunks = dims
    x = lax.axis_index("head")
    ctx = lax.axis_index("ctx")
    y = ctx // group
    j = lax.rem(ctx, group)
    base = y * group
    rows = s_send.shape[1]
    half_x = nx // 2
    half_c = chunks // 2
    width = chunks * LANE
    per_head = LANE // rows

    barrier = pltpu.get_barrier_semaphore()

    def greet_row(r, _):
        pl.semaphore_signal(
            barrier, inc=1, device_id={"ctx": base + lax.rem(j + r, group)}, device_id_type=MESH
        )
        return 0

    def greet_y(r, _):
        pl.semaphore_signal(
            barrier, inc=1, device_id={"ctx": lax.rem(y + r, ny) * group + j}, device_id_type=MESH
        )
        return 0

    def greet_x(r, _):
        pl.semaphore_signal(
            barrier, inc=1, device_id={"head": lax.rem(x + r, nx)}, device_id_type=MESH
        )
        return 0

    ld_in = pltpu.make_async_copy(ld_hbm, ld, in_sem.at[0])
    k_in = pltpu.make_async_copy(k_hbm, k, in_sem.at[1])
    v_in = pltpu.make_async_copy(v_hbm, v, in_sem.at[2])
    q_in = pltpu.make_async_copy(q_hbm, q, in_sem.at[3])
    gain_in = pltpu.make_async_copy(gain_hbm, gain, in_sem.at[4])
    for copy in (ld_in, k_in, v_in, q_in, gain_in):
        copy.start()
    lax.fori_loop(1, group, greet_row, 0)
    lax.fori_loop(1, ny, greet_y, 0)
    lax.fori_loop(1, nx, greet_x, 0)

    row_index = lax.broadcasted_iota(jnp.int32, (LANE, LANE), 0)
    col_index = lax.broadcasted_iota(jnp.int32, (LANE, LANE), 1)
    upper = jnp.where(row_index <= col_index, 1.0, 0.0).astype(F32)
    ld_in.wait()
    cum = jnp.dot(ld[...], upper, precision=HIGHEST, preferred_element_type=F32)
    for h in range(heads):
        spread = jnp.transpose(jnp.broadcast_to(cum[h : h + 1, :], (LANE, LANE)))
        cc[h] = spread
        d_send[h] = jnp.exp(spread[LANE - 1 : LANE, :])

    pl.semaphore_wait(barrier, (group - 1) + (ny - 1) + (nx - 1))

    def send_decay(r, _):
        owner = lax.rem(j + r, group)
        pltpu.make_async_remote_copy(
            src_ref=d_send.at[owner // per_head],
            dst_ref=d_recv.at[j],
            send_sem=d_sem.at[0],
            recv_sem=d_sem.at[1],
            device_id={"ctx": base + owner},
            device_id_type=MESH,
        ).start()
        return 0

    lax.fori_loop(1, group, send_decay, 0)
    d_recv[pl.ds(j, 1)] = d_send[pl.ds(j // per_head, 1)]

    k_in.wait()
    v_in.wait()
    for h in range(heads):
        columns = slice(h * LANE, (h + 1) * LANE)
        spread = cc[h]
        tail = jnp.exp(spread[LANE - 1 : LANE, :] - spread)
        faded = (k[:, columns].astype(F32) * tail).astype(BF16)
        state = lax.dot_general(
            faded, v[:, columns], (((0,), (0,)), ((), ())), preferred_element_type=F32
        )
        s_send[h * per_head : (h + 1) * per_head] = state.astype(BF16).reshape(per_head, rows, LANE)

        def send_slice(owner, _):
            @pl.when(owner != j)
            def _():
                pltpu.make_async_remote_copy(
                    src_ref=s_send.at[owner],
                    dst_ref=z_recv.at[j],
                    send_sem=z_sem.at[0],
                    recv_sem=z_sem.at[1],
                    device_id={"ctx": base + owner},
                    device_id_type=MESH,
                ).start()

            return 0

        lax.fori_loop(h * per_head, (h + 1) * per_head, send_slice, 0)
    z_recv[pl.ds(j, 1)] = s_send[pl.ds(j, 1)]

    def weight_copy(r):
        start = pl.multiple_of(lax.rem(x + r, nx) * width, LANE)
        return pltpu.make_async_copy(w_hbm.at[:, pl.ds(start, width)], w.at[r], w_sem.at[0])

    for step in range(half_x):
        distance = half_x - step
        for r in sorted({distance, nx - distance}):
            weight_copy(r).start()
    weight_copy(0).start()

    def bulk(ref, send_sem, recv_sem):
        return pltpu.make_async_remote_copy(
            src_ref=ref, dst_ref=ref, send_sem=send_sem, recv_sem=recv_sem,
            device_id={"head": lax.rem(x + 1, nx)}, device_id_type=MESH,
        )

    bulk(d_recv.at[pl.ds(0, group - 1)], d_sem.at[0], d_sem.at[1]).wait_recv()
    running = jnp.ones((1, LANE), F32)
    for i in range(group):
        pd_buf[i] = running
        running = running * d_recv[i]
    yd_send[0] = running

    def send_row_decay(r, _):
        pltpu.make_async_remote_copy(
            src_ref=yd_send.at[0],
            dst_ref=yd_recv.at[y],
            send_sem=yd_sem.at[0],
            recv_sem=yd_sem.at[1],
            device_id={"ctx": lax.rem(y + r, ny) * group + j},
            device_id_type=MESH,
        ).start()
        return 0

    if ny > 1:
        lax.fori_loop(1, ny, send_row_decay, 0)

    q_in.wait()
    causal = row_index >= col_index
    for h in range(heads):
        columns = slice(h * LANE, (h + 1) * LANE)
        spread = cc[h]
        scores = lax.dot_general(
            q[:, columns], k[:, columns], (((1,), (1,)), ((), ())), preferred_element_type=F32
        )
        differ = jnp.where(causal, spread - cum[h : h + 1, :], -1e30)
        weights = (jnp.exp(differ) * scores).astype(BF16)
        within[h] = jnp.dot(weights, v[:, columns], preferred_element_type=F32)
        cc[h] = jnp.exp(spread)

    bulk(z_recv.at[pl.ds(0, group - 1)], z_sem.at[0], z_sem.at[1]).wait_recv()
    carry = jnp.zeros((rows, LANE), F32)
    for i in range(group):
        e_buf[i] = carry
        carry = d_recv[i] * carry + z_recv[i].astype(F32)
    r_send[0] = carry.astype(BF16)

    def row_total(target):
        return pltpu.make_async_remote_copy(
            src_ref=r_send.at[0],
            dst_ref=y_recv.at[y],
            send_sem=y_send_sem.at[target],
            recv_sem=y_recv_sem.at[y],
            device_id={"ctx": target * group + j},
            device_id_type=MESH,
        )

    def send_total(target, _):
        row_total(target).start()
        return 0

    lax.fori_loop(y + 1, ny, send_total, 0)
    if ny > 1:
        bulk(yd_recv.at[pl.ds(0, ny - 1)], yd_sem.at[0], yd_sem.at[1]).wait_recv()

    def add_row(i, prefix):
        pltpu.make_async_remote_copy(
            src_ref=y_recv.at[i],
            dst_ref=y_recv.at[i],
            send_sem=y_send_sem.at[i],
            recv_sem=y_recv_sem.at[i],
            device_id={"ctx": i * group + j},
            device_id_type=MESH,
        ).wait_recv()
        return yd_recv[i] * prefix + y_recv[i].astype(F32)

    prefix = lax.fori_loop(0, y, add_row, jnp.zeros((rows, LANE), F32))

    def send_prefix(i, _):
        p_send[i] = (pd_buf[i] * prefix + e_buf[i]).astype(BF16)

        @pl.when(i != j)
        def _():
            pltpu.make_async_remote_copy(
                src_ref=p_send.at[i],
                dst_ref=s_in.at[j],
                send_sem=p_sem.at[0],
                recv_sem=p_sem.at[1],
                device_id={"ctx": base + i},
                device_id_type=MESH,
            ).start()

        return 0

    lax.fori_loop(0, group, send_prefix, 0)
    s_in[pl.ds(j, 1)] = p_send[pl.ds(j, 1)]

    gain_in.wait()
    pltpu.make_async_copy(w, w, w_sem.at[0]).wait()

    bulk(s_in.at[pl.ds(0, group - 1)], p_sem.at[0], p_sem.at[1]).wait_recv()
    squares = jnp.zeros((LANE, LANE), F32)
    for h in range(heads):
        columns = slice(h * LANE, (h + 1) * LANE)
        state = s_in[h * per_head : (h + 1) * per_head].reshape(LANE, LANE)
        carried = jnp.dot(q[:, columns], state, preferred_element_type=F32)
        attn = within[h] + cc[h] * carried
        squares = squares + attn * attn
        act[:, columns] = (attn * gain[:, columns]).astype(BF16)

    right, left = lax.rem(x + 1, nx), lax.rem(x + nx - 1, nx)

    def slot(step, c, way):
        if step == 0:
            return c if way == 0 else c - half_c
        return half_c + chunks * (step - 1) + c

    def hop(step, c, way):
        place = slot(step, c, way)
        return pltpu.make_async_remote_copy(
            src_ref=tx.at[way, place],
            dst_ref=rx.at[way, place],
            send_sem=tx_sem.at[way],
            recv_sem=rx_sem.at[way, place],
            device_id={"head": right if way == 0 else left},
            device_id_type=MESH,
        )

    def project(r, pair):
        return jnp.dot(
            act[...], w[r, :, pair * 2 * LANE : (pair + 1) * 2 * LANE], preferred_element_type=F32
        )

    for pair in sorted(range(chunks // 2), key=lambda p: min(p, chunks // 2 - 1 - p)):
        block = project(half_x, pair)
        for c in (2 * pair, 2 * pair + 1):
            way = 0 if c < half_c else 1
            part = block[:, :LANE] if c % 2 == 0 else block[:, LANE:]
            tx[way, slot(0, c, way)] = part.astype(BF16)
            hop(0, c, way).start()

    sq_send[0] = jnp.sum(jnp.transpose(squares), axis=0, keepdims=True)

    def send_squares(r, _):
        pltpu.make_async_remote_copy(
            src_ref=sq_send.at[0],
            dst_ref=sq_recv.at[x],
            send_sem=sq_sem.at[0],
            recv_sem=sq_sem.at[1],
            device_id={"head": lax.rem(x + r, nx)},
            device_id_type=MESH,
        ).start()
        return 0

    lax.fori_loop(1, nx, send_squares, 0)
    sq_recv[pl.ds(x, 1)] = sq_send[...]

    def arrives(step, c, way):
        if step == 0:
            return (c < half_c) == (way == 0)
        return True

    def fill(way, r):
        for pair in range(chunks // 2):
            block = project(r, pair)
            own[way, 2 * pair] = block[:, :LANE]
            own[way, 2 * pair + 1] = block[:, LANE:]

    for step in range(1, half_x):
        distance = half_x - step
        fill(0, distance)
        fill(1, nx - distance)
        order = [list(range(half_c, chunks)) + list(range(half_c)), list(range(chunks))]
        for place in range(chunks):
            for way in (0, 1):
                c = order[way][place]
                total = own[way, c]
                if arrives(step - 1, c, way):
                    hop(step - 1, c, way).wait_recv()
                    total = total + rx[way, slot(step - 1, c, way)].astype(F32)
                tx[way, slot(step, c, way)] = total.astype(BF16)
                hop(step, c, way).start()

    fill(0, 0)
    bulk(sq_recv.at[pl.ds(0, nx - 1)], sq_sem.at[0], sq_sem.at[1]).wait_recv()
    total = sq_recv[0]
    for i in range(1, nx):
        total = total + sq_recv[i]
    scale = lax.rsqrt(total / (nx * heads * LANE) + 1e-05)
    scale = jnp.transpose(jnp.broadcast_to(scale, (LANE, LANE)))
    for c in range(chunks):
        block = own[0, c]
        for way in (0, 1):
            if arrives(half_x - 1, c, way):
                hop(half_x - 1, c, way).wait_recv()
                block = block + rx[way, slot(half_x - 1, c, way)].astype(F32)
        out_ref[:, c * LANE : (c + 1) * LANE] = (block * scale).astype(BF16)

    bulk(d_recv.at[pl.ds(0, group - 1)], d_sem.at[0], d_sem.at[1]).wait_send()
    bulk(z_recv.at[pl.ds(0, group - 1)], z_sem.at[0], z_sem.at[1]).wait_send()
    if ny > 1:
        bulk(yd_recv.at[pl.ds(0, ny - 1)], yd_sem.at[0], yd_sem.at[1]).wait_send()
    bulk(s_in.at[pl.ds(0, group - 1)], p_sem.at[0], p_sem.at[1]).wait_send()
    bulk(sq_recv.at[pl.ds(0, nx - 1)], sq_sem.at[0], sq_sem.at[1]).wait_send()

    def left_total(target, _):
        row_total(target).wait_send()
        return 0

    lax.fori_loop(y + 1, ny, left_total, 0)
    for way in (0, 1):
        bulk(tx.at[way], tx_sem.at[way], rx_sem.at[way, 0]).wait_send()


def solution(mesh, group=ROW_GROUP):
    nx, ctx = mesh.shape["head"], mesh.shape["ctx"]
    ny = ctx // group

    def local(query, keys, values, log_decay, norm_gain, out_weight):
        tokens, features = query.shape
        heads = log_decay.shape[1]
        width = out_weight.shape[1] // nx
        chunks = width // LANE
        rows = features // group
        slots = chunks // 2 + chunks * (nx // 2 - 1)
        anywhere = pl.BlockSpec(memory_space=pl.ANY)
        square = (LANE, LANE)
        dma = pltpu.SemaphoreType.DMA
        return pl.pallas_call(
            functools.partial(body, (nx, ny, group, heads, chunks)),
            out_shape=pltpu.VMEM((tokens, width), BF16),
            in_specs=[anywhere] * 6,
            out_specs=pl.BlockSpec(memory_space=pltpu.VMEM),
            scratch_shapes=[
                pltpu.VMEM((tokens, features), BF16),
                pltpu.VMEM((tokens, features), BF16),
                pltpu.VMEM((tokens, features), BF16),
                pltpu.VMEM((heads, tokens), F32),
                pltpu.VMEM((1, features), F32),
                pltpu.VMEM((nx, features, width), BF16),
                pltpu.VMEM((heads,) + square, F32),
                pltpu.VMEM((heads,) + square, F32),
                pltpu.VMEM((tokens, features), BF16),
                pltpu.VMEM((heads, 1, LANE), F32),
                pltpu.VMEM((group, 1, LANE), F32),
                pltpu.VMEM((group, rows, LANE), BF16),
                pltpu.VMEM((group, rows, LANE), BF16),
                pltpu.VMEM((group, rows, LANE), F32),
                pltpu.VMEM((group, 1, LANE), F32),
                pltpu.VMEM((1, 1, LANE), F32),
                pltpu.VMEM((ny, 1, LANE), F32),
                pltpu.VMEM((1, rows, LANE), BF16),
                pltpu.VMEM((ny, rows, LANE), BF16),
                pltpu.VMEM((group, rows, LANE), BF16),
                pltpu.VMEM((group, rows, LANE), BF16),
                pltpu.VMEM((1, 1, LANE), F32),
                pltpu.VMEM((nx, 1, LANE), F32),
                pltpu.VMEM((2, chunks) + square, F32),
                pltpu.VMEM((2, slots) + square, BF16),
                pltpu.VMEM((2, slots) + square, BF16),
                dma((5,)),
                dma((1,)),
                dma((2,)),
                dma((2,)),
                dma((2,)),
                dma((ny,)),
                dma((ny,)),
                dma((2,)),
                dma((2,)),
                dma((2,)),
                dma((2, slots)),
            ],
            compiler_params=pltpu.CompilerParams(
                collective_id=0, has_side_effects=True, vmem_limit_bytes=60 * 2**20
            ),
        )(query, keys, values, log_decay.T, norm_gain.reshape(1, features), out_weight)

    placed = (
        P("ctx", "head"),
        P("ctx", "head"),
        P("ctx", "head"),
        P("ctx", "head"),
        P("head"),
        P("head", None),
    )
    return jax.shard_map(
        local, mesh=mesh, in_specs=placed, out_specs=P("ctx", "head"), check_vma=False
    )
```

```python
import functools

import jax
import jax.numpy as jnp
from jax import lax
from jax.experimental import pallas as pl
from jax.experimental.pallas import tpu as pltpu
from jax.sharding import PartitionSpec as P

MESH = pl.DeviceIdType.MESH
HIGHEST = lax.Precision.HIGHEST
LANE = 128
ROW_GROUP = 16
F32 = jnp.float32
BF16 = jnp.bfloat16


def body(
    dims,
    q_hbm, k_hbm, v_hbm, ld_hbm, gain_hbm, w_hbm,
    out_ref,
    q, k, v, ld, gain, w,
    cc, within, act,
    d_send, d_recv, s_send, z_recv, e_buf, pd_buf,
    yd_send, yd_recv, r_send, y_recv, p_send, s_in,
    sq_send, sq_recv, own, tx, rx,
    in_sem, w_sem, d_sem, z_sem, yd_send_sem, yd_recv_sem, y_send_sem, y_recv_sem, p_sem, sq_sem,
    tx_sem, rx_sem,
):
    nx, ny, group, heads, chunks = dims
    x = lax.axis_index("head")
    ctx = lax.axis_index("ctx")
    y = ctx // group
    j = lax.rem(ctx, group)
    base = y * group
    rows = s_send.shape[1]
    half_x = nx // 2
    half_c = chunks // 2
    width = chunks * LANE
    per_head = LANE // rows

    barrier = pltpu.get_barrier_semaphore()

    def greet_row(r, _):
        pl.semaphore_signal(
            barrier, inc=1, device_id={"ctx": base + lax.rem(j + r, group)}, device_id_type=MESH
        )
        return 0

    def greet_y(r, _):
        pl.semaphore_signal(
            barrier, inc=1, device_id={"ctx": lax.rem(y + r, ny) * group + j}, device_id_type=MESH
        )
        return 0

    def greet_x(r, _):
        pl.semaphore_signal(
            barrier, inc=1, device_id={"head": lax.rem(x + r, nx)}, device_id_type=MESH
        )
        return 0

    ld_in = pltpu.make_async_copy(ld_hbm, ld, in_sem.at[0])
    k_in = pltpu.make_async_copy(k_hbm, k, in_sem.at[1])
    v_in = pltpu.make_async_copy(v_hbm, v, in_sem.at[2])
    q_in = pltpu.make_async_copy(q_hbm, q, in_sem.at[3])
    gain_in = pltpu.make_async_copy(gain_hbm, gain, in_sem.at[4])
    for copy in (ld_in, k_in, v_in, q_in, gain_in):
        copy.start()
    lax.fori_loop(1, group, greet_row, 0)
    lax.fori_loop(1, ny, greet_y, 0)
    lax.fori_loop(1, nx, greet_x, 0)

    row_index = lax.broadcasted_iota(jnp.int32, (LANE, LANE), 0)
    col_index = lax.broadcasted_iota(jnp.int32, (LANE, LANE), 1)
    upper = jnp.where(row_index <= col_index, 1.0, 0.0).astype(F32)
    ld_in.wait()
    cum = jnp.dot(ld[...], upper, precision=HIGHEST, preferred_element_type=F32)
    for h in range(heads):
        spread = jnp.transpose(jnp.broadcast_to(cum[h : h + 1, :], (LANE, LANE)))
        cc[h] = spread
        d_send[h] = jnp.exp(spread[LANE - 1 : LANE, :])

    pl.semaphore_wait(barrier, (group - 1) + (ny - 1) + (nx - 1))

    def send_decay(r, _):
        owner = lax.rem(j + r, group)
        pltpu.make_async_remote_copy(
            src_ref=d_send.at[owner // per_head],
            dst_ref=d_recv.at[j],
            send_sem=d_sem.at[0],
            recv_sem=d_sem.at[1],
            device_id={"ctx": base + owner},
            device_id_type=MESH,
        ).start()
        return 0

    lax.fori_loop(1, group, send_decay, 0)
    d_recv[pl.ds(j, 1)] = d_send[pl.ds(j // per_head, 1)]

    k_in.wait()
    v_in.wait()
    for h in range(heads):
        columns = slice(h * LANE, (h + 1) * LANE)
        spread = cc[h]
        tail = jnp.exp(spread[LANE - 1 : LANE, :] - spread)
        faded = (k[:, columns].astype(F32) * tail).astype(BF16)
        state = lax.dot_general(
            faded, v[:, columns], (((0,), (0,)), ((), ())), preferred_element_type=F32
        )
        s_send[h * per_head : (h + 1) * per_head] = state.astype(BF16).reshape(per_head, rows, LANE)

        def send_slice(owner, _):
            @pl.when(owner != j)
            def _():
                pltpu.make_async_remote_copy(
                    src_ref=s_send.at[owner],
                    dst_ref=z_recv.at[j],
                    send_sem=z_sem.at[0],
                    recv_sem=z_sem.at[1],
                    device_id={"ctx": base + owner},
                    device_id_type=MESH,
                ).start()

            return 0

        lax.fori_loop(h * per_head, (h + 1) * per_head, send_slice, 0)
    z_recv[pl.ds(j, 1)] = s_send[pl.ds(j, 1)]

    def weight_copy(r):
        start = pl.multiple_of(lax.rem(x + r, nx) * width, LANE)
        return pltpu.make_async_copy(w_hbm.at[:, pl.ds(start, width)], w.at[r], w_sem.at[0])

    for step in range(half_x):
        distance = half_x - step
        for r in sorted({distance, nx - distance}):
            weight_copy(r).start()
    weight_copy(0).start()

    q_in.wait()
    causal = row_index >= col_index
    for h in range(heads):
        columns = slice(h * LANE, (h + 1) * LANE)
        spread = cc[h]
        scores = lax.dot_general(
            q[:, columns], k[:, columns], (((1,), (1,)), ((), ())), preferred_element_type=F32
        )
        differ = jnp.where(causal, spread - cum[h : h + 1, :], -1e30)
        weights = (jnp.exp(differ) * scores).astype(BF16)
        within[h] = jnp.dot(weights, v[:, columns], preferred_element_type=F32)
        cc[h] = jnp.exp(spread)

    def bulk(ref, send_sem, recv_sem):
        return pltpu.make_async_remote_copy(
            src_ref=ref, dst_ref=ref, send_sem=send_sem, recv_sem=recv_sem,
            device_id={"head": lax.rem(x + 1, nx)}, device_id_type=MESH,
        )

    bulk(d_recv.at[pl.ds(0, group - 1)], d_sem.at[0], d_sem.at[1]).wait_recv()
    running = jnp.ones((1, LANE), F32)
    for i in range(group):
        pd_buf[i] = running
        running = running * d_recv[i]
    yd_send[0] = running

    def row_decay(target):
        return pltpu.make_async_remote_copy(
            src_ref=yd_send.at[0],
            dst_ref=yd_recv.at[y],
            send_sem=yd_send_sem.at[target],
            recv_sem=yd_recv_sem.at[y],
            device_id={"ctx": target * group + j},
            device_id_type=MESH,
        )

    offsets = sorted(range(1, ny), key=lambda r: -min(r, ny - r))

    def each_later(act_on):
        for r in offsets:
            @pl.when(y + r < ny)
            def _():
                act_on(y + r)

    each_later(lambda target: row_decay(target).start())

    bulk(z_recv.at[pl.ds(0, group - 1)], z_sem.at[0], z_sem.at[1]).wait_recv()
    carry = jnp.zeros((rows, LANE), F32)
    for i in range(group):
        e_buf[i] = carry
        carry = d_recv[i] * carry + z_recv[i].astype(F32)
    r_send[0] = carry.astype(BF16)

    def row_total(target):
        return pltpu.make_async_remote_copy(
            src_ref=r_send.at[0],
            dst_ref=y_recv.at[y],
            send_sem=y_send_sem.at[target],
            recv_sem=y_recv_sem.at[y],
            device_id={"ctx": target * group + j},
            device_id_type=MESH,
        )

    each_later(lambda target: row_total(target).start())

    def add_row(i, prefix):
        pltpu.make_async_remote_copy(
            src_ref=y_recv.at[i],
            dst_ref=y_recv.at[i],
            send_sem=y_send_sem.at[i],
            recv_sem=y_recv_sem.at[i],
            device_id={"ctx": i * group + j},
            device_id_type=MESH,
        ).wait_recv()
        pltpu.make_async_remote_copy(
            src_ref=yd_recv.at[i],
            dst_ref=yd_recv.at[i],
            send_sem=yd_send_sem.at[i],
            recv_sem=yd_recv_sem.at[i],
            device_id={"ctx": i * group + j},
            device_id_type=MESH,
        ).wait_recv()
        return yd_recv[i] * prefix + y_recv[i].astype(F32)

    prefix = lax.fori_loop(0, y, add_row, jnp.zeros((rows, LANE), F32))

    def send_prefix(i, _):
        p_send[i] = (pd_buf[i] * prefix + e_buf[i]).astype(BF16)

        @pl.when(i != j)
        def _():
            pltpu.make_async_remote_copy(
                src_ref=p_send.at[i],
                dst_ref=s_in.at[j],
                send_sem=p_sem.at[0],
                recv_sem=p_sem.at[1],
                device_id={"ctx": base + i},
                device_id_type=MESH,
            ).start()

        return 0

    lax.fori_loop(0, group, send_prefix, 0)
    s_in[pl.ds(j, 1)] = p_send[pl.ds(j, 1)]

    gain_in.wait()
    pltpu.make_async_copy(w, w, w_sem.at[0]).wait()

    bulk(s_in.at[pl.ds(0, group - 1)], p_sem.at[0], p_sem.at[1]).wait_recv()
    squares = jnp.zeros((LANE, LANE), F32)
    for h in range(heads):
        columns = slice(h * LANE, (h + 1) * LANE)
        state = s_in[h * per_head : (h + 1) * per_head].reshape(LANE, LANE)
        carried = jnp.dot(q[:, columns], state, preferred_element_type=F32)
        attn = within[h] + cc[h] * carried
        squares = squares + attn * attn
        act[:, columns] = (attn * gain[:, columns]).astype(BF16)

    right, left = lax.rem(x + 1, nx), lax.rem(x + nx - 1, nx)

    def slot(step, c, way):
        if step == 0:
            return c if way == 0 else c - half_c
        return half_c + chunks * (step - 1) + c

    def hop(step, c, way):
        place = slot(step, c, way)
        return pltpu.make_async_remote_copy(
            src_ref=tx.at[way, place],
            dst_ref=rx.at[way, place],
            send_sem=tx_sem.at[way],
            recv_sem=rx_sem.at[way, place],
            device_id={"head": right if way == 0 else left},
            device_id_type=MESH,
        )

    def project(r, pair):
        return jnp.dot(
            act[...], w[r, :, pair * 2 * LANE : (pair + 1) * 2 * LANE], preferred_element_type=F32
        )

    for pair in sorted(range(chunks // 2), key=lambda p: min(p, chunks // 2 - 1 - p)):
        block = project(half_x, pair)
        for c in (2 * pair, 2 * pair + 1):
            way = 0 if c < half_c else 1
            part = block[:, :LANE] if c % 2 == 0 else block[:, LANE:]
            tx[way, slot(0, c, way)] = part.astype(BF16)
            hop(0, c, way).start()

    sq_send[0] = jnp.sum(jnp.transpose(squares), axis=0, keepdims=True)

    def send_squares(r, _):
        pltpu.make_async_remote_copy(
            src_ref=sq_send.at[0],
            dst_ref=sq_recv.at[x],
            send_sem=sq_sem.at[0],
            recv_sem=sq_sem.at[1],
            device_id={"head": lax.rem(x + r, nx)},
            device_id_type=MESH,
        ).start()
        return 0

    lax.fori_loop(1, nx, send_squares, 0)
    sq_recv[pl.ds(x, 1)] = sq_send[...]

    def arrives(step, c, way):
        if step == 0:
            return (c < half_c) == (way == 0)
        return True

    def fill(way, r):
        for pair in range(chunks // 2):
            block = project(r, pair)
            own[way, 2 * pair] = block[:, :LANE]
            own[way, 2 * pair + 1] = block[:, LANE:]

    for step in range(1, half_x):
        distance = half_x - step
        fill(0, distance)
        fill(1, nx - distance)
        order = [list(range(half_c, chunks)) + list(range(half_c)), list(range(chunks))]
        for place in range(chunks):
            for way in (0, 1):
                c = order[way][place]
                total = own[way, c]
                if arrives(step - 1, c, way):
                    hop(step - 1, c, way).wait_recv()
                    total = total + rx[way, slot(step - 1, c, way)].astype(F32)
                tx[way, slot(step, c, way)] = total.astype(BF16)
                hop(step, c, way).start()

    fill(0, 0)
    bulk(sq_recv.at[pl.ds(0, nx - 1)], sq_sem.at[0], sq_sem.at[1]).wait_recv()
    total = sq_recv[0]
    for i in range(1, nx):
        total = total + sq_recv[i]
    scale = lax.rsqrt(total / (nx * heads * LANE) + 1e-05)
    scale = jnp.transpose(jnp.broadcast_to(scale, (LANE, LANE)))
    for c in range(chunks):
        block = own[0, c]
        for way in (0, 1):
            if arrives(half_x - 1, c, way):
                hop(half_x - 1, c, way).wait_recv()
                block = block + rx[way, slot(half_x - 1, c, way)].astype(F32)
        out_ref[:, c * LANE : (c + 1) * LANE] = (block * scale).astype(BF16)

    bulk(d_recv.at[pl.ds(0, group - 1)], d_sem.at[0], d_sem.at[1]).wait_send()
    bulk(z_recv.at[pl.ds(0, group - 1)], z_sem.at[0], z_sem.at[1]).wait_send()
    bulk(s_in.at[pl.ds(0, group - 1)], p_sem.at[0], p_sem.at[1]).wait_send()
    bulk(sq_recv.at[pl.ds(0, nx - 1)], sq_sem.at[0], sq_sem.at[1]).wait_send()

    def departed(target):
        row_total(target).wait_send()
        row_decay(target).wait_send()

    each_later(departed)
    for way in (0, 1):
        bulk(tx.at[way], tx_sem.at[way], rx_sem.at[way, 0]).wait_send()


def solution(mesh, group=ROW_GROUP):
    nx, ctx = mesh.shape["head"], mesh.shape["ctx"]
    ny = ctx // group

    def local(query, keys, values, log_decay, norm_gain, out_weight):
        tokens, features = query.shape
        heads = log_decay.shape[1]
        width = out_weight.shape[1] // nx
        chunks = width // LANE
        rows = features // group
        slots = chunks // 2 + chunks * (nx // 2 - 1)
        anywhere = pl.BlockSpec(memory_space=pl.ANY)
        square = (LANE, LANE)
        dma = pltpu.SemaphoreType.DMA
        return pl.pallas_call(
            functools.partial(body, (nx, ny, group, heads, chunks)),
            out_shape=pltpu.VMEM((tokens, width), BF16),
            in_specs=[anywhere] * 6,
            out_specs=pl.BlockSpec(memory_space=pltpu.VMEM),
            scratch_shapes=[
                pltpu.VMEM((tokens, features), BF16),
                pltpu.VMEM((tokens, features), BF16),
                pltpu.VMEM((tokens, features), BF16),
                pltpu.VMEM((heads, tokens), F32),
                pltpu.VMEM((1, features), F32),
                pltpu.VMEM((nx, features, width), BF16),
                pltpu.VMEM((heads,) + square, F32),
                pltpu.VMEM((heads,) + square, F32),
                pltpu.VMEM((tokens, features), BF16),
                pltpu.VMEM((heads, 1, LANE), F32),
                pltpu.VMEM((group, 1, LANE), F32),
                pltpu.VMEM((group, rows, LANE), BF16),
                pltpu.VMEM((group, rows, LANE), BF16),
                pltpu.VMEM((group, rows, LANE), F32),
                pltpu.VMEM((group, 1, LANE), F32),
                pltpu.VMEM((1, 1, LANE), F32),
                pltpu.VMEM((ny, 1, LANE), F32),
                pltpu.VMEM((1, rows, LANE), BF16),
                pltpu.VMEM((ny, rows, LANE), BF16),
                pltpu.VMEM((group, rows, LANE), BF16),
                pltpu.VMEM((group, rows, LANE), BF16),
                pltpu.VMEM((1, 1, LANE), F32),
                pltpu.VMEM((nx, 1, LANE), F32),
                pltpu.VMEM((2, chunks) + square, F32),
                pltpu.VMEM((2, slots) + square, BF16),
                pltpu.VMEM((2, slots) + square, BF16),
                dma((5,)),
                dma((1,)),
                dma((2,)),
                dma((2,)),
                dma((ny,)),
                dma((ny,)),
                dma((ny,)),
                dma((ny,)),
                dma((2,)),
                dma((2,)),
                dma((2,)),
                dma((2, slots)),
            ],
            compiler_params=pltpu.CompilerParams(
                collective_id=0, has_side_effects=True, vmem_limit_bytes=60 * 2**20
            ),
        )(query, keys, values, log_decay.T, norm_gain.reshape(1, features), out_weight)

    placed = (
        P("ctx", "head"),
        P("ctx", "head"),
        P("ctx", "head"),
        P("ctx", "head"),
        P("head"),
        P("head", None),
    )
    return jax.shard_map(
        local, mesh=mesh, in_specs=placed, out_specs=P("ctx", "head"), check_vma=False
    )
```

```python
import functools

import jax
import jax.numpy as jnp
from jax import lax
from jax.experimental import pallas as pl
from jax.experimental.pallas import tpu as pltpu
from jax.sharding import PartitionSpec as P

MESH = pl.DeviceIdType.MESH
HIGHEST = lax.Precision.HIGHEST
LANE = 128
ROW_GROUP = 16
F32 = jnp.float32
BF16 = jnp.bfloat16


def body(
    dims,
    q_hbm, k_hbm, v_hbm, ld_hbm, gain_hbm, w_hbm,
    out_ref,
    q, k, v, ld, gain, w,
    cc, within, act,
    d_send, d_recv, s_send, z_recv, e_buf, pd_buf,
    yd_send, yd_recv, r_send, y_recv, p_send, s_in,
    sq_send, sq_recv, own, tx, rx,
    in_sem, w_sem, d_sem, z_sem, sent_sem, yd_send_sem, yd_recv_sem, y_send_sem, y_recv_sem, p_sem, sq_sem,
    tx_sem, rx_sem,
):
    nx, ny, group, heads, chunks = dims
    x = lax.axis_index("head")
    ctx = lax.axis_index("ctx")
    y = ctx // group
    j = lax.rem(ctx, group)
    base = y * group
    rows = s_send.shape[1]
    half_x = nx // 2
    half_c = chunks // 2
    width = chunks * LANE
    per_head = LANE // rows
    slices = heads * per_head
    nz = group // 2

    z_at, core = j // 2, lax.rem(j, 2)
    far = z_at // (nz // 2)
    rank = far * (z_at - (nz - 3)) + (1 - far) * (2 - z_at)

    def owner_of(s):
        level, near = min(s // 4, 2), (s // 2) % 2
        z_owner = 2 - level if near else nz - 3 + level
        return 2 * z_owner + s % 2, s // 4 - level

    def slice_of(slot):
        return 4 * (rank + slot) + 2 * (1 - far) + core

    def owning(slot, act_on):
        pl.when(rank >= 2 * slot)(functools.partial(act_on, slot))

    def exchanged(act_on):
        pl.when(rank == 2)(functools.partial(act_on, slices - 2))
        pl.when((rank >= 0) & (rank < 2))(functools.partial(act_on, slices - 1))
        pl.when(rank < 0)(functools.partial(act_on, slices))

    barrier = pltpu.get_barrier_semaphore()

    def greet_row(r, _):
        pl.semaphore_signal(
            barrier, inc=1, device_id={"ctx": base + lax.rem(j + r, group)}, device_id_type=MESH
        )
        return 0

    def greet_y(r, _):
        pl.semaphore_signal(
            barrier, inc=1, device_id={"ctx": lax.rem(y + r, ny) * group + j}, device_id_type=MESH
        )
        return 0

    def greet_x(r, _):
        pl.semaphore_signal(
            barrier, inc=1, device_id={"head": lax.rem(x + r, nx)}, device_id_type=MESH
        )
        return 0

    ld_in = pltpu.make_async_copy(ld_hbm, ld, in_sem.at[0])
    k_in = pltpu.make_async_copy(k_hbm, k, in_sem.at[1])
    v_in = pltpu.make_async_copy(v_hbm, v, in_sem.at[2])
    q_in = pltpu.make_async_copy(q_hbm, q, in_sem.at[3])
    gain_in = pltpu.make_async_copy(gain_hbm, gain, in_sem.at[4])
    for copy in (ld_in, k_in, v_in, q_in, gain_in):
        copy.start()
    lax.fori_loop(1, group, greet_row, 0)
    lax.fori_loop(1, ny, greet_y, 0)
    lax.fori_loop(1, nx, greet_x, 0)

    row_index = lax.broadcasted_iota(jnp.int32, (LANE, LANE), 0)
    col_index = lax.broadcasted_iota(jnp.int32, (LANE, LANE), 1)
    upper = jnp.where(row_index <= col_index, 1.0, 0.0).astype(F32)
    ld_in.wait()
    cum = jnp.dot(ld[...], upper, precision=HIGHEST, preferred_element_type=F32)
    for h in range(heads):
        spread = jnp.transpose(jnp.broadcast_to(cum[h : h + 1, :], (LANE, LANE)))
        cc[h] = spread
        d_send[h] = jnp.exp(spread[LANE - 1 : LANE, :])

    pl.semaphore_wait(barrier, (group - 1) + (ny - 1) + (nx - 1))

    def to_owner(s, src, dst, send_sem, recv_sem):
        owner, slot = owner_of(s)

        @pl.when(owner != j)
        def _():
            pltpu.make_async_remote_copy(
                src_ref=src,
                dst_ref=dst.at[slot, j],
                send_sem=send_sem,
                recv_sem=recv_sem.at[slot],
                device_id={"ctx": base + owner},
                device_id_type=MESH,
            ).start()

    for s in range(slices):
        to_owner(s, d_send.at[s // per_head], d_recv, sent_sem.at[0], d_sem)

    def keep_decay(slot):
        d_recv[slot, pl.ds(j, 1)] = d_send[pl.ds(slice_of(slot) // per_head, 1)]

    owning(0, keep_decay)
    owning(1, keep_decay)

    k_in.wait()
    v_in.wait()
    for h in range(heads):
        columns = slice(h * LANE, (h + 1) * LANE)
        spread = cc[h]
        tail = jnp.exp(spread[LANE - 1 : LANE, :] - spread)
        faded = (k[:, columns].astype(F32) * tail).astype(BF16)
        state = lax.dot_general(
            faded, v[:, columns], (((0,), (0,)), ((), ())), preferred_element_type=F32
        )
        s_send[h * per_head : (h + 1) * per_head] = state.astype(BF16).reshape(per_head, rows, LANE)

        for s in range(h * per_head, (h + 1) * per_head):
            to_owner(s, s_send.at[s], z_recv, sent_sem.at[1], z_sem)

    def keep_slice(slot):
        z_recv[slot, pl.ds(j, 1)] = s_send[pl.ds(slice_of(slot), 1)]

    owning(0, keep_slice)
    owning(1, keep_slice)

    def weight_copy(r):
        start = pl.multiple_of(lax.rem(x + r, nx) * width, LANE)
        return pltpu.make_async_copy(w_hbm.at[:, pl.ds(start, width)], w.at[r], w_sem.at[0])

    for step in range(half_x):
        distance = half_x - step
        for r in sorted({distance, nx - distance}):
            weight_copy(r).start()
    weight_copy(0).start()

    q_in.wait()
    causal = row_index >= col_index
    for h in range(heads):
        columns = slice(h * LANE, (h + 1) * LANE)
        spread = cc[h]
        scores = lax.dot_general(
            q[:, columns], k[:, columns], (((1,), (1,)), ((), ())), preferred_element_type=F32
        )
        differ = jnp.where(causal, spread - cum[h : h + 1, :], -1e30)
        weights = (jnp.exp(differ) * scores).astype(BF16)
        within[h] = jnp.dot(weights, v[:, columns], preferred_element_type=F32)
        cc[h] = jnp.exp(spread)

    def bulk(ref, send_sem, recv_sem):
        return pltpu.make_async_remote_copy(
            src_ref=ref, dst_ref=ref, send_sem=send_sem, recv_sem=recv_sem,
            device_id={"head": lax.rem(x + 1, nx)}, device_id_type=MESH,
        )

    def row_decay(slot, target):
        return pltpu.make_async_remote_copy(
            src_ref=yd_send.at[slot],
            dst_ref=yd_recv.at[slot, y],
            send_sem=yd_send_sem.at[slot, target],
            recv_sem=yd_recv_sem.at[slot, y],
            device_id={"ctx": target * group + j},
            device_id_type=MESH,
        )

    def row_total(slot, target):
        return pltpu.make_async_remote_copy(
            src_ref=r_send.at[slot],
            dst_ref=y_recv.at[slot, y],
            send_sem=y_send_sem.at[slot, target],
            recv_sem=y_recv_sem.at[slot, y],
            device_id={"ctx": target * group + j},
            device_id_type=MESH,
        )

    offsets = sorted(range(1, ny), key=lambda r: -min(r, ny - r))

    def each_later(act_on):
        for r in offsets:
            @pl.when(y + r < ny)
            def _():
                act_on(y + r)

    def fold_decays(slot):
        bulk(d_recv.at[slot, pl.ds(0, group - 1)], sent_sem.at[0], d_sem.at[slot]).wait_recv()
        running = jnp.ones((1, LANE), F32)
        for i in range(group):
            pd_buf[slot, i] = running
            running = running * d_recv[slot, i]
        yd_send[slot] = running
        each_later(lambda target: row_decay(slot, target).start())

    def scan_row(slot):
        bulk(z_recv.at[slot, pl.ds(0, group - 1)], sent_sem.at[1], z_sem.at[slot]).wait_recv()
        carry = jnp.zeros((rows, LANE), F32)
        for i in range(group):
            e_buf[slot, i] = carry
            carry = d_recv[slot, i] * carry + z_recv[slot, i].astype(F32)
        r_send[slot] = carry.astype(BF16)
        each_later(lambda target: row_total(slot, target).start())

    def prefixes(slot):
        def add_row(i, prefix):
            for ref, send_sem, recv_sem in (
                (y_recv, y_send_sem, y_recv_sem), (yd_recv, yd_send_sem, yd_recv_sem)
            ):
                bulk(ref.at[slot, i], send_sem.at[slot, i], recv_sem.at[slot, i]).wait_recv()
            return yd_recv[slot, i] * prefix + y_recv[slot, i].astype(F32)

        prefix = lax.fori_loop(0, y, add_row, jnp.zeros((rows, LANE), F32))
        mine = slice_of(slot)

        def send_prefix(i, _):
            p_send[slot, i] = (pd_buf[slot, i] * prefix + e_buf[slot, i]).astype(BF16)

            @pl.when(i != j)
            def _():
                pltpu.make_async_remote_copy(
                    src_ref=p_send.at[slot, i],
                    dst_ref=s_in.at[mine],
                    send_sem=sent_sem.at[2 + slot],
                    recv_sem=p_sem.at[0],
                    device_id={"ctx": base + i},
                    device_id_type=MESH,
                ).start()

            return 0

        lax.fori_loop(0, group, send_prefix, 0)
        s_in[pl.ds(mine, 1)] = p_send[slot, pl.ds(j, 1)]

    for stage in (fold_decays, scan_row, prefixes):
        owning(0, stage)
        owning(1, stage)

    gain_in.wait()
    pltpu.make_async_copy(w, w, w_sem.at[0]).wait()

    exchanged(lambda count: bulk(s_in.at[pl.ds(0, count)], sent_sem.at[2], p_sem.at[0]).wait_recv())
    squares = jnp.zeros((LANE, LANE), F32)
    for h in range(heads):
        columns = slice(h * LANE, (h + 1) * LANE)
        state = s_in[h * per_head : (h + 1) * per_head].reshape(LANE, LANE)
        carried = jnp.dot(q[:, columns], state, preferred_element_type=F32)
        attn = within[h] + cc[h] * carried
        squares = squares + attn * attn
        act[:, columns] = (attn * gain[:, columns]).astype(BF16)

    right, left = lax.rem(x + 1, nx), lax.rem(x + nx - 1, nx)

    def slot(step, c, way):
        if step == 0:
            return c if way == 0 else c - half_c
        return half_c + chunks * (step - 1) + c

    def hop(step, c, way):
        place = slot(step, c, way)
        return pltpu.make_async_remote_copy(
            src_ref=tx.at[way, place],
            dst_ref=rx.at[way, place],
            send_sem=tx_sem.at[way],
            recv_sem=rx_sem.at[way, place],
            device_id={"head": right if way == 0 else left},
            device_id_type=MESH,
        )

    def project(r, pair):
        return jnp.dot(
            act[...], w[r, :, pair * 2 * LANE : (pair + 1) * 2 * LANE], preferred_element_type=F32
        )

    for pair in sorted(range(chunks // 2), key=lambda p: min(p, chunks // 2 - 1 - p)):
        block = project(half_x, pair)
        for c in (2 * pair, 2 * pair + 1):
            way = 0 if c < half_c else 1
            part = block[:, :LANE] if c % 2 == 0 else block[:, LANE:]
            tx[way, slot(0, c, way)] = part.astype(BF16)
            hop(0, c, way).start()

    sq_send[0] = jnp.sum(jnp.transpose(squares), axis=0, keepdims=True)

    def send_squares(r, _):
        pltpu.make_async_remote_copy(
            src_ref=sq_send.at[0],
            dst_ref=sq_recv.at[x],
            send_sem=sq_sem.at[0],
            recv_sem=sq_sem.at[1],
            device_id={"head": lax.rem(x + r, nx)},
            device_id_type=MESH,
        ).start()
        return 0

    lax.fori_loop(1, nx, send_squares, 0)
    sq_recv[pl.ds(x, 1)] = sq_send[...]

    def arrives(step, c, way):
        if step == 0:
            return (c < half_c) == (way == 0)
        return True

    def fill(way, r):
        for pair in range(chunks // 2):
            block = project(r, pair)
            own[way, 2 * pair] = block[:, :LANE]
            own[way, 2 * pair + 1] = block[:, LANE:]

    for step in range(1, half_x):
        distance = half_x - step
        fill(0, distance)
        fill(1, nx - distance)
        order = [list(range(half_c, chunks)) + list(range(half_c)), list(range(chunks))]
        for place in range(chunks):
            for way in (0, 1):
                c = order[way][place]
                total = own[way, c]
                if arrives(step - 1, c, way):
                    hop(step - 1, c, way).wait_recv()
                    total = total + rx[way, slot(step - 1, c, way)].astype(F32)
                tx[way, slot(step, c, way)] = total.astype(BF16)
                hop(step, c, way).start()

    fill(0, 0)
    bulk(sq_recv.at[pl.ds(0, nx - 1)], sq_sem.at[0], sq_sem.at[1]).wait_recv()
    total = sq_recv[0]
    for i in range(1, nx):
        total = total + sq_recv[i]
    scale = lax.rsqrt(total / (nx * heads * LANE) + 1e-05)
    scale = jnp.transpose(jnp.broadcast_to(scale, (LANE, LANE)))
    for c in range(chunks):
        block = own[0, c]
        for way in (0, 1):
            if arrives(half_x - 1, c, way):
                hop(half_x - 1, c, way).wait_recv()
                block = block + rx[way, slot(half_x - 1, c, way)].astype(F32)
        out_ref[:, c * LANE : (c + 1) * LANE] = (block * scale).astype(BF16)

    def slices_left(count):
        bulk(pd_buf.at[0, pl.ds(0, count)], sent_sem.at[0], d_sem.at[0]).wait_send()
        bulk(s_send.at[pl.ds(0, count)], sent_sem.at[1], z_sem.at[0]).wait_send()

    exchanged(slices_left)

    def owner_left(slot):
        bulk(p_send.at[slot, pl.ds(0, group - 1)], sent_sem.at[2 + slot], p_sem.at[0]).wait_send()

        def departed(target):
            row_total(slot, target).wait_send()
            row_decay(slot, target).wait_send()

        each_later(departed)

    owning(0, owner_left)
    owning(1, owner_left)
    bulk(sq_recv.at[pl.ds(0, nx - 1)], sq_sem.at[0], sq_sem.at[1]).wait_send()
    for way in (0, 1):
        bulk(tx.at[way], tx_sem.at[way], rx_sem.at[way, 0]).wait_send()


def solution(mesh, group=ROW_GROUP):
    nx, ctx = mesh.shape["head"], mesh.shape["ctx"]
    ny = ctx // group

    def local(query, keys, values, log_decay, norm_gain, out_weight):
        tokens, features = query.shape
        heads = log_decay.shape[1]
        width = out_weight.shape[1] // nx
        chunks = width // LANE
        rows = features // 16
        slots = chunks // 2 + chunks * (nx // 2 - 1)
        anywhere = pl.BlockSpec(memory_space=pl.ANY)
        square = (LANE, LANE)
        dma = pltpu.SemaphoreType.DMA
        return pl.pallas_call(
            functools.partial(body, (nx, ny, group, heads, chunks)),
            out_shape=pltpu.VMEM((tokens, width), BF16),
            in_specs=[anywhere] * 6,
            out_specs=pl.BlockSpec(memory_space=pltpu.VMEM),
            scratch_shapes=[
                pltpu.VMEM((tokens, features), BF16),
                pltpu.VMEM((tokens, features), BF16),
                pltpu.VMEM((tokens, features), BF16),
                pltpu.VMEM((heads, tokens), F32),
                pltpu.VMEM((1, features), F32),
                pltpu.VMEM((nx, features, width), BF16),
                pltpu.VMEM((heads,) + square, F32),
                pltpu.VMEM((heads,) + square, F32),
                pltpu.VMEM((tokens, features), BF16),
                pltpu.VMEM((heads, 1, LANE), F32),
                pltpu.VMEM((2, group, 1, LANE), F32),
                pltpu.VMEM((16, rows, LANE), BF16),
                pltpu.VMEM((2, group, rows, LANE), BF16),
                pltpu.VMEM((2, group, rows, LANE), F32),
                pltpu.VMEM((2, group, 1, LANE), F32),
                pltpu.VMEM((2, 1, LANE), F32),
                pltpu.VMEM((2, ny, 1, LANE), F32),
                pltpu.VMEM((2, rows, LANE), BF16),
                pltpu.VMEM((2, ny, rows, LANE), BF16),
                pltpu.VMEM((2, group, rows, LANE), BF16),
                pltpu.VMEM((16, rows, LANE), BF16),
                pltpu.VMEM((1, 1, LANE), F32),
                pltpu.VMEM((nx, 1, LANE), F32),
                pltpu.VMEM((2, chunks) + square, F32),
                pltpu.VMEM((2, slots) + square, BF16),
                pltpu.VMEM((2, slots) + square, BF16),
                dma((5,)),
                dma((1,)),
                dma((2,)),
                dma((2,)),
                dma((4,)),
                dma((2, ny)),
                dma((2, ny)),
                dma((2, ny)),
                dma((2, ny)),
                dma((1,)),
                dma((2,)),
                dma((2,)),
                dma((2, slots)),
            ],
            compiler_params=pltpu.CompilerParams(
                collective_id=0, has_side_effects=True, vmem_limit_bytes=60 * 2**20
            ),
        )(query, keys, values, log_decay.T, norm_gain.reshape(1, features), out_weight)

    placed = (
        P("ctx", "head"),
        P("ctx", "head"),
        P("ctx", "head"),
        P("ctx", "head"),
        P("head"),
        P("head", None),
    )
    return jax.shard_map(
        local, mesh=mesh, in_specs=placed, out_specs=P("ctx", "head"), check_vma=False
    )
```

```python
import functools

import jax
import jax.numpy as jnp
from jax import lax
from jax.experimental import pallas as pl
from jax.experimental.pallas import tpu as pltpu
from jax.sharding import PartitionSpec as P

MESH = pl.DeviceIdType.MESH
HIGHEST = lax.Precision.HIGHEST
LANE = 128
ROW_GROUP = 16
F32 = jnp.float32
BF16 = jnp.bfloat16


def body(
    dims,
    q_hbm, k_hbm, v_hbm, ld_hbm, gain_hbm, w_hbm,
    out_ref,
    q, k, v, ld, gain, w,
    cc, within, act,
    d_send, d_recv, s_send, z_recv, e_buf, pd_buf,
    yd_send, yd_recv, r_send, y_recv, p_send, s_in,
    sq_send, sq_recv, own, tx, rx,
    in_sem, w_sem, d_sem, z_sem, yd_send_sem, yd_recv_sem, y_send_sem, y_recv_sem, p_sem, sq_sem,
    tx_sem, rx_sem,
):
    nx, ny, group, heads, chunks = dims
    x = lax.axis_index("head")
    ctx = lax.axis_index("ctx")
    y = ctx // group
    j = lax.rem(ctx, group)
    base = y * group
    rows = s_send.shape[1]
    half_x = nx // 2
    half_c = chunks // 2
    width = chunks * LANE
    per_head = LANE // rows

    barrier = pltpu.get_barrier_semaphore()

    def greet_row(r, _):
        pl.semaphore_signal(
            barrier, inc=1, device_id={"ctx": base + lax.rem(j + r, group)}, device_id_type=MESH
        )
        return 0

    def greet_y(r, _):
        pl.semaphore_signal(
            barrier, inc=1, device_id={"ctx": lax.rem(y + r, ny) * group + j}, device_id_type=MESH
        )
        return 0

    def greet_x(r, _):
        pl.semaphore_signal(
            barrier, inc=1, device_id={"head": lax.rem(x + r, nx)}, device_id_type=MESH
        )
        return 0

    ld_in = pltpu.make_async_copy(ld_hbm, ld, in_sem.at[0])
    k_in = pltpu.make_async_copy(k_hbm, k, in_sem.at[1])
    v_in = pltpu.make_async_copy(v_hbm, v, in_sem.at[2])
    q_in = pltpu.make_async_copy(q_hbm, q, in_sem.at[3])
    gain_in = pltpu.make_async_copy(gain_hbm, gain, in_sem.at[4])
    for copy in (ld_in, k_in, v_in, q_in, gain_in):
        copy.start()
    offsets = sorted(range(1, ny), key=lambda r: -min(r, ny - r))
    for r in offsets:
        greet_y(r, 0)
    for r in sorted(range(1, nx), key=lambda r: -min(r, nx - r)):
        greet_x(r, 0)
    lax.fori_loop(1, group, greet_row, 0)

    row_index = lax.broadcasted_iota(jnp.int32, (LANE, LANE), 0)
    col_index = lax.broadcasted_iota(jnp.int32, (LANE, LANE), 1)
    upper = jnp.where(row_index <= col_index, 1.0, 0.0).astype(F32)
    ld_in.wait()
    cum = jnp.dot(ld[...], upper, precision=HIGHEST, preferred_element_type=F32)
    for h in range(heads):
        spread = jnp.transpose(jnp.broadcast_to(cum[h : h + 1, :], (LANE, LANE)))
        cc[h] = spread
        d_send[h] = jnp.exp(spread[LANE - 1 : LANE, :])

    k_in.wait()
    v_in.wait()
    for h in range(heads):
        columns = slice(h * LANE, (h + 1) * LANE)
        spread = cc[h]
        tail = jnp.exp(spread[LANE - 1 : LANE, :] - spread)
        faded = (k[:, columns].astype(F32) * tail).astype(BF16)
        state = lax.dot_general(
            faded, v[:, columns], (((0,), (0,)), ((), ())), preferred_element_type=F32
        )
        s_send[h * per_head : (h + 1) * per_head] = state.astype(BF16).reshape(per_head, rows, LANE)

    pl.semaphore_wait(barrier, (group - 1) + (ny - 1) + (nx - 1))

    for r in sorted(range(1, group), key=lambda r: -min(r, group - r)):
        owner = lax.rem(j + r, group)
        for src, dst, sem in (
            (d_send.at[owner // per_head], d_recv, d_sem), (s_send.at[owner], z_recv, z_sem)
        ):
            pltpu.make_async_remote_copy(
                src_ref=src,
                dst_ref=dst.at[j],
                send_sem=sem.at[0],
                recv_sem=sem.at[1],
                device_id={"ctx": base + owner},
                device_id_type=MESH,
            ).start()
    d_recv[pl.ds(j, 1)] = d_send[pl.ds(j // per_head, 1)]
    z_recv[pl.ds(j, 1)] = s_send[pl.ds(j, 1)]

    def weight_copy(r):
        start = pl.multiple_of(lax.rem(x + r, nx) * width, LANE)
        return pltpu.make_async_copy(w_hbm.at[:, pl.ds(start, width)], w.at[r], w_sem.at[0])

    for step in range(half_x):
        distance = half_x - step
        for r in sorted({distance, nx - distance}):
            weight_copy(r).start()
    weight_copy(0).start()

    q_in.wait()
    causal = row_index >= col_index
    for h in range(heads):
        columns = slice(h * LANE, (h + 1) * LANE)
        spread = cc[h]
        scores = lax.dot_general(
            q[:, columns], k[:, columns], (((1,), (1,)), ((), ())), preferred_element_type=F32
        )
        differ = jnp.where(causal, spread - cum[h : h + 1, :], -1e30)
        weights = (jnp.exp(differ) * scores).astype(BF16)
        within[h] = jnp.dot(weights, v[:, columns], preferred_element_type=F32)
        cc[h] = jnp.exp(spread)

    def bulk(ref, send_sem, recv_sem):
        return pltpu.make_async_remote_copy(
            src_ref=ref, dst_ref=ref, send_sem=send_sem, recv_sem=recv_sem,
            device_id={"head": lax.rem(x + 1, nx)}, device_id_type=MESH,
        )

    bulk(d_recv.at[pl.ds(0, group - 1)], d_sem.at[0], d_sem.at[1]).wait_recv()
    running = jnp.ones((1, LANE), F32)
    for i in range(group):
        pd_buf[i] = running
        running = running * d_recv[i]
    yd_send[0] = running

    def row_decay(target):
        return pltpu.make_async_remote_copy(
            src_ref=yd_send.at[0],
            dst_ref=yd_recv.at[y],
            send_sem=yd_send_sem.at[target],
            recv_sem=yd_recv_sem.at[y],
            device_id={"ctx": target * group + j},
            device_id_type=MESH,
        )

    def each_later(act_on):
        for r in offsets:
            @pl.when(y + r < ny)
            def _():
                act_on(y + r)

    each_later(lambda target: row_decay(target).start())

    bulk(z_recv.at[pl.ds(0, group - 1)], z_sem.at[0], z_sem.at[1]).wait_recv()
    carry = jnp.zeros((rows, LANE), F32)
    for i in range(group):
        e_buf[i] = carry
        carry = d_recv[i] * carry + z_recv[i].astype(F32)
    r_send[0] = carry.astype(BF16)

    def row_total(target):
        return pltpu.make_async_remote_copy(
            src_ref=r_send.at[0],
            dst_ref=y_recv.at[y],
            send_sem=y_send_sem.at[target],
            recv_sem=y_recv_sem.at[y],
            device_id={"ctx": target * group + j},
            device_id_type=MESH,
        )

    each_later(lambda target: row_total(target).start())

    def add_row(i, prefix):
        pltpu.make_async_remote_copy(
            src_ref=y_recv.at[i],
            dst_ref=y_recv.at[i],
            send_sem=y_send_sem.at[i],
            recv_sem=y_recv_sem.at[i],
            device_id={"ctx": i * group + j},
            device_id_type=MESH,
        ).wait_recv()
        pltpu.make_async_remote_copy(
            src_ref=yd_recv.at[i],
            dst_ref=yd_recv.at[i],
            send_sem=yd_send_sem.at[i],
            recv_sem=yd_recv_sem.at[i],
            device_id={"ctx": i * group + j},
            device_id_type=MESH,
        ).wait_recv()
        return yd_recv[i] * prefix + y_recv[i].astype(F32)

    prefix = lax.fori_loop(0, y, add_row, jnp.zeros((rows, LANE), F32))

    def send_prefix(i, _):
        p_send[i] = (pd_buf[i] * prefix + e_buf[i]).astype(BF16)

        @pl.when(i != j)
        def _():
            pltpu.make_async_remote_copy(
                src_ref=p_send.at[i],
                dst_ref=s_in.at[j],
                send_sem=p_sem.at[0],
                recv_sem=p_sem.at[1],
                device_id={"ctx": base + i},
                device_id_type=MESH,
            ).start()

        return 0

    lax.fori_loop(0, group, send_prefix, 0)
    s_in[pl.ds(j, 1)] = p_send[pl.ds(j, 1)]

    gain_in.wait()
    pltpu.make_async_copy(w, w, w_sem.at[0]).wait()

    bulk(s_in.at[pl.ds(0, group - 1)], p_sem.at[0], p_sem.at[1]).wait_recv()
    squares = jnp.zeros((LANE, LANE), F32)
    for h in range(heads):
        columns = slice(h * LANE, (h + 1) * LANE)
        state = s_in[h * per_head : (h + 1) * per_head].reshape(LANE, LANE)
        carried = jnp.dot(q[:, columns], state, preferred_element_type=F32)
        attn = within[h] + cc[h] * carried
        squares = squares + attn * attn
        act[:, columns] = (attn * gain[:, columns]).astype(BF16)

    right, left = lax.rem(x + 1, nx), lax.rem(x + nx - 1, nx)

    def slot(step, c, way):
        if step == 0:
            return c if way == 0 else c - half_c
        return half_c + chunks * (step - 1) + c

    def hop(step, c, way):
        place = slot(step, c, way)
        return pltpu.make_async_remote_copy(
            src_ref=tx.at[way, place],
            dst_ref=rx.at[way, place],
            send_sem=tx_sem.at[way],
            recv_sem=rx_sem.at[way, place],
            device_id={"head": right if way == 0 else left},
            device_id_type=MESH,
        )

    def project(r, pair):
        return jnp.dot(
            act[...], w[r, :, pair * 2 * LANE : (pair + 1) * 2 * LANE], preferred_element_type=F32
        )

    for pair in sorted(range(chunks // 2), key=lambda p: min(p, chunks // 2 - 1 - p)):
        block = project(half_x, pair)
        for c in (2 * pair, 2 * pair + 1):
            way = 0 if c < half_c else 1
            part = block[:, :LANE] if c % 2 == 0 else block[:, LANE:]
            tx[way, slot(0, c, way)] = part.astype(BF16)
            hop(0, c, way).start()

    sq_send[0] = jnp.sum(jnp.transpose(squares), axis=0, keepdims=True)

    def send_squares(r, _):
        pltpu.make_async_remote_copy(
            src_ref=sq_send.at[0],
            dst_ref=sq_recv.at[x],
            send_sem=sq_sem.at[0],
            recv_sem=sq_sem.at[1],
            device_id={"head": lax.rem(x + r, nx)},
            device_id_type=MESH,
        ).start()
        return 0

    lax.fori_loop(1, nx, send_squares, 0)
    sq_recv[pl.ds(x, 1)] = sq_send[...]

    def arrives(step, c, way):
        if step == 0:
            return (c < half_c) == (way == 0)
        return True

    def fill(way, r):
        for pair in range(chunks // 2):
            block = project(r, pair)
            own[way, 2 * pair] = block[:, :LANE]
            own[way, 2 * pair + 1] = block[:, LANE:]

    for step in range(1, half_x):
        distance = half_x - step
        fill(0, distance)
        fill(1, nx - distance)
        order = [list(range(half_c, chunks)) + list(range(half_c)), list(range(chunks))]
        for place in range(chunks):
            for way in (0, 1):
                c = order[way][place]
                total = own[way, c]
                if arrives(step - 1, c, way):
                    hop(step - 1, c, way).wait_recv()
                    total = total + rx[way, slot(step - 1, c, way)].astype(F32)
                tx[way, slot(step, c, way)] = total.astype(BF16)
                hop(step, c, way).start()

    fill(0, 0)
    bulk(sq_recv.at[pl.ds(0, nx - 1)], sq_sem.at[0], sq_sem.at[1]).wait_recv()
    total = sq_recv[0]
    for i in range(1, nx):
        total = total + sq_recv[i]
    scale = lax.rsqrt(total / (nx * heads * LANE) + 1e-05)
    scale = jnp.transpose(jnp.broadcast_to(scale, (LANE, LANE)))
    for c in range(chunks):
        block = own[0, c]
        for way in (0, 1):
            if arrives(half_x - 1, c, way):
                hop(half_x - 1, c, way).wait_recv()
                block = block + rx[way, slot(half_x - 1, c, way)].astype(F32)
        out_ref[:, c * LANE : (c + 1) * LANE] = (block * scale).astype(BF16)

    bulk(d_recv.at[pl.ds(0, group - 1)], d_sem.at[0], d_sem.at[1]).wait_send()
    bulk(z_recv.at[pl.ds(0, group - 1)], z_sem.at[0], z_sem.at[1]).wait_send()
    bulk(s_in.at[pl.ds(0, group - 1)], p_sem.at[0], p_sem.at[1]).wait_send()
    bulk(sq_recv.at[pl.ds(0, nx - 1)], sq_sem.at[0], sq_sem.at[1]).wait_send()

    def departed(target):
        row_total(target).wait_send()
        row_decay(target).wait_send()

    each_later(departed)
    for way in (0, 1):
        bulk(tx.at[way], tx_sem.at[way], rx_sem.at[way, 0]).wait_send()


def solution(mesh, group=ROW_GROUP):
    nx, ctx = mesh.shape["head"], mesh.shape["ctx"]
    ny = ctx // group

    def local(query, keys, values, log_decay, norm_gain, out_weight):
        tokens, features = query.shape
        heads = log_decay.shape[1]
        width = out_weight.shape[1] // nx
        chunks = width // LANE
        rows = features // group
        slots = chunks // 2 + chunks * (nx // 2 - 1)
        anywhere = pl.BlockSpec(memory_space=pl.ANY)
        square = (LANE, LANE)
        dma = pltpu.SemaphoreType.DMA
        return pl.pallas_call(
            functools.partial(body, (nx, ny, group, heads, chunks)),
            out_shape=pltpu.VMEM((tokens, width), BF16),
            in_specs=[anywhere] * 6,
            out_specs=pl.BlockSpec(memory_space=pltpu.VMEM),
            scratch_shapes=[
                pltpu.VMEM((tokens, features), BF16),
                pltpu.VMEM((tokens, features), BF16),
                pltpu.VMEM((tokens, features), BF16),
                pltpu.VMEM((heads, tokens), F32),
                pltpu.VMEM((1, features), F32),
                pltpu.VMEM((nx, features, width), BF16),
                pltpu.VMEM((heads,) + square, F32),
                pltpu.VMEM((heads,) + square, F32),
                pltpu.VMEM((tokens, features), BF16),
                pltpu.VMEM((heads, 1, LANE), F32),
                pltpu.VMEM((group, 1, LANE), F32),
                pltpu.VMEM((group, rows, LANE), BF16),
                pltpu.VMEM((group, rows, LANE), BF16),
                pltpu.VMEM((group, rows, LANE), F32),
                pltpu.VMEM((group, 1, LANE), F32),
                pltpu.VMEM((1, 1, LANE), F32),
                pltpu.VMEM((ny, 1, LANE), F32),
                pltpu.VMEM((1, rows, LANE), BF16),
                pltpu.VMEM((ny, rows, LANE), BF16),
                pltpu.VMEM((group, rows, LANE), BF16),
                pltpu.VMEM((group, rows, LANE), BF16),
                pltpu.VMEM((1, 1, LANE), F32),
                pltpu.VMEM((nx, 1, LANE), F32),
                pltpu.VMEM((2, chunks) + square, F32),
                pltpu.VMEM((2, slots) + square, BF16),
                pltpu.VMEM((2, slots) + square, BF16),
                dma((5,)),
                dma((1,)),
                dma((2,)),
                dma((2,)),
                dma((ny,)),
                dma((ny,)),
                dma((ny,)),
                dma((ny,)),
                dma((2,)),
                dma((2,)),
                dma((2,)),
                dma((2, slots)),
            ],
            compiler_params=pltpu.CompilerParams(
                collective_id=0, has_side_effects=True, vmem_limit_bytes=60 * 2**20
            ),
        )(query, keys, values, log_decay.T, norm_gain.reshape(1, features), out_weight)

    placed = (
        P("ctx", "head"),
        P("ctx", "head"),
        P("ctx", "head"),
        P("ctx", "head"),
        P("head"),
        P("head", None),
    )
    return jax.shard_map(
        local, mesh=mesh, in_specs=placed, out_specs=P("ctx", "head"), check_vma=False
    )
```

```python
import functools

import jax
import jax.numpy as jnp
from jax import lax
from jax.experimental import pallas as pl
from jax.experimental.pallas import tpu as pltpu
from jax.sharding import PartitionSpec as P

MESH = pl.DeviceIdType.MESH
HIGHEST = lax.Precision.HIGHEST
LANE = 128
ROW_GROUP = 16
F32 = jnp.float32
BF16 = jnp.bfloat16


def body(
    dims,
    q_hbm, k_hbm, v_hbm, ld_hbm, gain_hbm, w_hbm,
    out_ref,
    q, k, v, ld, gain, w,
    cc, within, act,
    d_send, d_recv, s_send, z_recv, e_buf, pd_buf,
    yd_send, yd_recv, r_send, y_recv, p_send, s_in,
    sq_send, sq_recv, own, tx, rx,
    in_sem, w_sem, d_sem, z_sem, yd_send_sem, yd_recv_sem, y_send_sem, y_recv_sem, p_sem, sq_sem,
    tx_sem, rx_sem,
):
    nx, ny, group, heads, chunks = dims
    x = lax.axis_index("head")
    ctx = lax.axis_index("ctx")
    y = ctx // group
    j = lax.rem(ctx, group)
    base = y * group
    rows = s_send.shape[1]
    half_x = nx // 2
    half_c = chunks // 2
    width = chunks * LANE
    per_head = LANE // rows

    barrier = pltpu.get_barrier_semaphore()

    def greet_row(r, _):
        pl.semaphore_signal(
            barrier, inc=1, device_id={"ctx": base + lax.rem(j + r, group)}, device_id_type=MESH
        )
        return 0

    def greet_y(r, _):
        pl.semaphore_signal(
            barrier, inc=1, device_id={"ctx": lax.rem(y + r, ny) * group + j}, device_id_type=MESH
        )
        return 0

    def greet_x(r, _):
        pl.semaphore_signal(
            barrier, inc=1, device_id={"head": lax.rem(x + r, nx)}, device_id_type=MESH
        )
        return 0

    ld_in = pltpu.make_async_copy(ld_hbm, ld, in_sem.at[0])
    k_in = pltpu.make_async_copy(k_hbm, k, in_sem.at[1])
    v_in = pltpu.make_async_copy(v_hbm, v, in_sem.at[2])
    q_in = pltpu.make_async_copy(q_hbm, q, in_sem.at[3])
    gain_in = pltpu.make_async_copy(gain_hbm, gain, in_sem.at[4])
    for copy in (ld_in, k_in, v_in, q_in, gain_in):
        copy.start()
    offsets = sorted(range(1, ny), key=lambda r: -min(r, ny - r))
    for r in offsets:
        greet_y(r, 0)
    for r in sorted(range(1, nx), key=lambda r: -min(r, nx - r)):
        greet_x(r, 0)
    lax.fori_loop(1, group, greet_row, 0)

    row_index = lax.broadcasted_iota(jnp.int32, (LANE, LANE), 0)
    col_index = lax.broadcasted_iota(jnp.int32, (LANE, LANE), 1)
    upper = jnp.where(row_index <= col_index, 1.0, 0.0).astype(F32)
    ld_in.wait()
    cum = jnp.dot(ld[...], upper, precision=HIGHEST, preferred_element_type=F32)
    for h in range(heads):
        spread = jnp.transpose(jnp.broadcast_to(cum[h : h + 1, :], (LANE, LANE)))
        cc[h] = spread
        d_send[h] = jnp.exp(spread[LANE - 1 : LANE, :])

    k_in.wait()
    v_in.wait()
    for h in range(heads):
        columns = slice(h * LANE, (h + 1) * LANE)
        spread = cc[h]
        tail = jnp.exp(spread[LANE - 1 : LANE, :] - spread)
        faded = (k[:, columns].astype(F32) * tail).astype(BF16)
        state = lax.dot_general(
            faded, v[:, columns], (((0,), (0,)), ((), ())), preferred_element_type=F32
        )
        s_send[h * per_head : (h + 1) * per_head] = state.astype(BF16).reshape(per_head, rows, LANE)

    pl.semaphore_wait(barrier, (group - 1) + (ny - 1) + (nx - 1))

    for r in sorted(range(1, group), key=lambda r: -min(r, group - r)):
        owner = lax.rem(j + r, group)
        for src, dst, sem in (
            (d_send.at[owner // per_head], d_recv, d_sem), (s_send.at[owner], z_recv, z_sem)
        ):
            pltpu.make_async_remote_copy(
                src_ref=src,
                dst_ref=dst.at[j],
                send_sem=sem.at[0],
                recv_sem=sem.at[1],
                device_id={"ctx": base + owner},
                device_id_type=MESH,
            ).start()
    d_recv[pl.ds(j, 1)] = d_send[pl.ds(j // per_head, 1)]
    z_recv[pl.ds(j, 1)] = s_send[pl.ds(j, 1)]

    def weight_copy(r):
        start = pl.multiple_of(lax.rem(x + r, nx) * width, LANE)
        return pltpu.make_async_copy(w_hbm.at[:, pl.ds(start, width)], w.at[r], w_sem.at[0])

    for step in range(half_x):
        distance = half_x - step
        for r in sorted({distance, nx - distance}):
            weight_copy(r).start()
    weight_copy(0).start()

    q_in.wait()
    causal = row_index >= col_index
    for h in range(heads):
        columns = slice(h * LANE, (h + 1) * LANE)
        spread = cc[h]
        scores = lax.dot_general(
            q[:, columns], k[:, columns], (((1,), (1,)), ((), ())), preferred_element_type=F32
        )
        differ = jnp.where(causal, spread - cum[h : h + 1, :], -1e30)
        weights = (jnp.exp(differ) * scores).astype(BF16)
        within[h] = jnp.dot(weights, v[:, columns], preferred_element_type=F32)
        cc[h] = jnp.exp(spread)

    def bulk(ref, send_sem, recv_sem):
        return pltpu.make_async_remote_copy(
            src_ref=ref, dst_ref=ref, send_sem=send_sem, recv_sem=recv_sem,
            device_id={"head": lax.rem(x + 1, nx)}, device_id_type=MESH,
        )

    bulk(d_recv.at[pl.ds(0, group - 1)], d_sem.at[0], d_sem.at[1]).wait_recv()
    running = jnp.ones((1, LANE), F32)
    for i in range(group):
        pd_buf[i] = running
        running = running * d_recv[i]
    yd_send[0] = running

    def row_decay(target):
        return pltpu.make_async_remote_copy(
            src_ref=yd_send.at[0],
            dst_ref=yd_recv.at[y],
            send_sem=yd_send_sem.at[target],
            recv_sem=yd_recv_sem.at[y],
            device_id={"ctx": target * group + j},
            device_id_type=MESH,
        )

    def each_later(act_on):
        for r in offsets:
            @pl.when(y + r < ny)
            def _():
                act_on(y + r)

    each_later(lambda target: row_decay(target).start())

    bulk(z_recv.at[pl.ds(0, group - 1)], z_sem.at[0], z_sem.at[1]).wait_recv()
    carry = jnp.zeros((rows, LANE), F32)
    for i in range(group):
        e_buf[i] = carry
        carry = d_recv[i] * carry + z_recv[i].astype(F32)
    r_send[0] = carry.astype(BF16)

    def row_total(target):
        return pltpu.make_async_remote_copy(
            src_ref=r_send.at[0],
            dst_ref=y_recv.at[y],
            send_sem=y_send_sem.at[target],
            recv_sem=y_recv_sem.at[y],
            device_id={"ctx": target * group + j},
            device_id_type=MESH,
        )

    each_later(lambda target: row_total(target).start())

    def add_row(i, prefix):
        pltpu.make_async_remote_copy(
            src_ref=y_recv.at[i],
            dst_ref=y_recv.at[i],
            send_sem=y_send_sem.at[i],
            recv_sem=y_recv_sem.at[i],
            device_id={"ctx": i * group + j},
            device_id_type=MESH,
        ).wait_recv()
        pltpu.make_async_remote_copy(
            src_ref=yd_recv.at[i],
            dst_ref=yd_recv.at[i],
            send_sem=yd_send_sem.at[i],
            recv_sem=yd_recv_sem.at[i],
            device_id={"ctx": i * group + j},
            device_id_type=MESH,
        ).wait_recv()
        return yd_recv[i] * prefix + y_recv[i].astype(F32)

    prefix = lax.fori_loop(0, y, add_row, jnp.zeros((rows, LANE), F32))

    def send_prefix(i, _):
        p_send[i] = (pd_buf[i] * prefix + e_buf[i]).astype(BF16)

        @pl.when(i != j)
        def _():
            pltpu.make_async_remote_copy(
                src_ref=p_send.at[i],
                dst_ref=s_in.at[j],
                send_sem=p_sem.at[0],
                recv_sem=p_sem.at[1],
                device_id={"ctx": base + i},
                device_id_type=MESH,
            ).start()

        return 0

    lax.fori_loop(0, group, send_prefix, 0)
    s_in[pl.ds(j, 1)] = p_send[pl.ds(j, 1)]

    gain_in.wait()
    pltpu.make_async_copy(w, w, w_sem.at[0]).wait()

    bulk(s_in.at[pl.ds(0, group - 1)], p_sem.at[0], p_sem.at[1]).wait_recv()
    squares = jnp.zeros((LANE, LANE), F32)
    for h in range(heads):
        columns = slice(h * LANE, (h + 1) * LANE)
        state = s_in[h * per_head : (h + 1) * per_head].reshape(LANE, LANE)
        carried = jnp.dot(q[:, columns], state, preferred_element_type=F32)
        attn = within[h] + cc[h] * carried
        squares = squares + attn * attn
        act[:, columns] = (attn * gain[:, columns]).astype(BF16)

    right, left = lax.rem(x + 1, nx), lax.rem(x + nx - 1, nx)

    def slot(step, c, way):
        if step == 0:
            return c if way == 0 else c - half_c
        return half_c + chunks * (step - 1) + c

    def hop(step, c, way):
        place = slot(step, c, way)
        return pltpu.make_async_remote_copy(
            src_ref=tx.at[way, place],
            dst_ref=rx.at[way, place],
            send_sem=tx_sem.at[way],
            recv_sem=rx_sem.at[way, place],
            device_id={"head": right if way == 0 else left},
            device_id_type=MESH,
        )

    def project(r, pair):
        return jnp.dot(
            act[...], w[r, :, pair * 2 * LANE : (pair + 1) * 2 * LANE], preferred_element_type=F32
        )

    for pair in sorted(range(chunks // 2), key=lambda p: min(p, chunks // 2 - 1 - p)):
        block = project(half_x, pair)
        for c in (2 * pair, 2 * pair + 1):
            way = 0 if c < half_c else 1
            part = block[:, :LANE] if c % 2 == 0 else block[:, LANE:]
            tx[way, slot(0, c, way)] = part.astype(BF16)
            hop(0, c, way).start()

    sq_send[0] = jnp.sum(jnp.transpose(squares), axis=0, keepdims=True)

    def send_squares(r, _):
        pltpu.make_async_remote_copy(
            src_ref=sq_send.at[0],
            dst_ref=sq_recv.at[x],
            send_sem=sq_sem.at[0],
            recv_sem=sq_sem.at[1],
            device_id={"head": lax.rem(x + r, nx)},
            device_id_type=MESH,
        ).start()
        return 0

    lax.fori_loop(1, nx, send_squares, 0)
    sq_recv[pl.ds(x, 1)] = sq_send[...]

    def arrives(step, c, way):
        if step == 0:
            return (c < half_c) == (way == 0)
        return True

    def fill(step, way, r):
        for pair in range(chunks // 2):
            block = project(r, pair)
            own[2 * step + way, 2 * pair] = block[:, :LANE]
            own[2 * step + way, 2 * pair + 1] = block[:, LANE:]

    def forward(step, c, way):
        total = own[2 * step + way, c]
        if arrives(step - 1, c, way):
            hop(step - 1, c, way).wait_recv()
            total = total + rx[way, slot(step - 1, c, way)].astype(F32)
        tx[way, slot(step, c, way)] = total.astype(BF16)
        hop(step, c, way).start()

    order = [list(range(half_c, chunks)) + list(range(half_c)), list(range(chunks))]
    for step in range(1, half_x):
        distance = half_x - step
        fill(step, 0, distance)
        fill(step, 1, nx - distance)
        if step == 1:
            for place in range(half_c):
                for way in (0, 1):
                    forward(1, order[way][place], way)
    fill(0, 0, 0)
    for step in range(1, half_x):
        for place in range(half_c if step == 1 else 0, chunks):
            for way in (0, 1):
                forward(step, order[way][place], way)

    bulk(sq_recv.at[pl.ds(0, nx - 1)], sq_sem.at[0], sq_sem.at[1]).wait_recv()
    total = sq_recv[0]
    for i in range(1, nx):
        total = total + sq_recv[i]
    scale = lax.rsqrt(total / (nx * heads * LANE) + 1e-05)
    scale = jnp.transpose(jnp.broadcast_to(scale, (LANE, LANE)))
    for c in range(chunks):
        block = own[0, c]
        for way in (0, 1):
            if arrives(half_x - 1, c, way):
                hop(half_x - 1, c, way).wait_recv()
                block = block + rx[way, slot(half_x - 1, c, way)].astype(F32)
        out_ref[:, c * LANE : (c + 1) * LANE] = (block * scale).astype(BF16)

    bulk(d_recv.at[pl.ds(0, group - 1)], d_sem.at[0], d_sem.at[1]).wait_send()
    bulk(z_recv.at[pl.ds(0, group - 1)], z_sem.at[0], z_sem.at[1]).wait_send()
    bulk(s_in.at[pl.ds(0, group - 1)], p_sem.at[0], p_sem.at[1]).wait_send()
    bulk(sq_recv.at[pl.ds(0, nx - 1)], sq_sem.at[0], sq_sem.at[1]).wait_send()

    def departed(target):
        row_total(target).wait_send()
        row_decay(target).wait_send()

    each_later(departed)
    for way in (0, 1):
        bulk(tx.at[way], tx_sem.at[way], rx_sem.at[way, 0]).wait_send()


def solution(mesh, group=ROW_GROUP):
    nx, ctx = mesh.shape["head"], mesh.shape["ctx"]
    ny = ctx // group

    def local(query, keys, values, log_decay, norm_gain, out_weight):
        tokens, features = query.shape
        heads = log_decay.shape[1]
        width = out_weight.shape[1] // nx
        chunks = width // LANE
        rows = features // group
        slots = chunks // 2 + chunks * (nx // 2 - 1)
        anywhere = pl.BlockSpec(memory_space=pl.ANY)
        square = (LANE, LANE)
        dma = pltpu.SemaphoreType.DMA
        return pl.pallas_call(
            functools.partial(body, (nx, ny, group, heads, chunks)),
            out_shape=pltpu.VMEM((tokens, width), BF16),
            in_specs=[anywhere] * 6,
            out_specs=pl.BlockSpec(memory_space=pltpu.VMEM),
            scratch_shapes=[
                pltpu.VMEM((tokens, features), BF16),
                pltpu.VMEM((tokens, features), BF16),
                pltpu.VMEM((tokens, features), BF16),
                pltpu.VMEM((heads, tokens), F32),
                pltpu.VMEM((1, features), F32),
                pltpu.VMEM((nx, features, width), BF16),
                pltpu.VMEM((heads,) + square, F32),
                pltpu.VMEM((heads,) + square, F32),
                pltpu.VMEM((tokens, features), BF16),
                pltpu.VMEM((heads, 1, LANE), F32),
                pltpu.VMEM((group, 1, LANE), F32),
                pltpu.VMEM((group, rows, LANE), BF16),
                pltpu.VMEM((group, rows, LANE), BF16),
                pltpu.VMEM((group, rows, LANE), F32),
                pltpu.VMEM((group, 1, LANE), F32),
                pltpu.VMEM((1, 1, LANE), F32),
                pltpu.VMEM((ny, 1, LANE), F32),
                pltpu.VMEM((1, rows, LANE), BF16),
                pltpu.VMEM((ny, rows, LANE), BF16),
                pltpu.VMEM((group, rows, LANE), BF16),
                pltpu.VMEM((group, rows, LANE), BF16),
                pltpu.VMEM((1, 1, LANE), F32),
                pltpu.VMEM((nx, 1, LANE), F32),
                pltpu.VMEM((nx, chunks) + square, F32),
                pltpu.VMEM((2, slots) + square, BF16),
                pltpu.VMEM((2, slots) + square, BF16),
                dma((5,)),
                dma((1,)),
                dma((2,)),
                dma((2,)),
                dma((ny,)),
                dma((ny,)),
                dma((ny,)),
                dma((ny,)),
                dma((2,)),
                dma((2,)),
                dma((2,)),
                dma((2, slots)),
            ],
            compiler_params=pltpu.CompilerParams(
                collective_id=0, has_side_effects=True, vmem_limit_bytes=60 * 2**20
            ),
        )(query, keys, values, log_decay.T, norm_gain.reshape(1, features), out_weight)

    placed = (
        P("ctx", "head"),
        P("ctx", "head"),
        P("ctx", "head"),
        P("ctx", "head"),
        P("head"),
        P("head", None),
    )
    return jax.shard_map(
        local, mesh=mesh, in_specs=placed, out_specs=P("ctx", "head"), check_vma=False
    )
```

```python
import functools

import jax
import jax.numpy as jnp
from jax import lax
from jax.experimental import pallas as pl
from jax.experimental.pallas import tpu as pltpu
from jax.sharding import PartitionSpec as P

MESH = pl.DeviceIdType.MESH
HIGHEST = lax.Precision.HIGHEST
LANE = 128
ROW_GROUP = 16
F32 = jnp.float32
BF16 = jnp.bfloat16


def body(
    dims,
    q_hbm, k_hbm, v_hbm, ld_hbm, gain_hbm, w_hbm,
    out_ref,
    q, k, v, ld, gain, w,
    cc, within, act,
    d_send, d_recv, s_send, z_recv, e_buf, pd_buf,
    yd_send, yd_recv, r_send, y_recv, p_send, s_in,
    sq_send, sq_recv, own, tx, rx,
    in_sem, w_sem, d_sem, z_sem, yd_send_sem, yd_recv_sem, y_send_sem, y_recv_sem, p_sem, sq_sem,
    tx_sem, rx_sem,
):
    nx, ny, group, heads, chunks = dims
    x = lax.axis_index("head")
    ctx = lax.axis_index("ctx")
    y = ctx // group
    j = lax.rem(ctx, group)
    base = y * group
    rows = s_send.shape[1]
    half_x = nx // 2
    half_c = chunks // 2
    width = chunks * LANE
    per_head = LANE // rows

    barrier = pltpu.get_barrier_semaphore()

    def greet_row(r, _):
        pl.semaphore_signal(
            barrier, inc=1, device_id={"ctx": base + lax.rem(j + r, group)}, device_id_type=MESH
        )
        return 0

    def greet_y(r, _):
        pl.semaphore_signal(
            barrier, inc=1, device_id={"ctx": lax.rem(y + r, ny) * group + j}, device_id_type=MESH
        )
        return 0

    def greet_x(r, _):
        pl.semaphore_signal(
            barrier, inc=1, device_id={"head": lax.rem(x + r, nx)}, device_id_type=MESH
        )
        return 0

    ld_in = pltpu.make_async_copy(ld_hbm, ld, in_sem.at[0])
    k_in = pltpu.make_async_copy(k_hbm, k, in_sem.at[1])
    v_in = pltpu.make_async_copy(v_hbm, v, in_sem.at[2])
    q_in = pltpu.make_async_copy(q_hbm, q, in_sem.at[3])
    gain_in = pltpu.make_async_copy(gain_hbm, gain, in_sem.at[4])
    for copy in (ld_in, k_in, v_in, q_in, gain_in):
        copy.start()
    offsets = sorted(range(1, ny), key=lambda r: -min(r, ny - r))
    for r in offsets:
        greet_y(r, 0)
    for r in sorted(range(1, nx), key=lambda r: -min(r, nx - r)):
        greet_x(r, 0)
    lax.fori_loop(1, group, greet_row, 0)

    row_index = lax.broadcasted_iota(jnp.int32, (LANE, LANE), 0)
    col_index = lax.broadcasted_iota(jnp.int32, (LANE, LANE), 1)
    upper = jnp.where(row_index <= col_index, 1.0, 0.0).astype(F32)
    ld_in.wait()
    cum = jnp.dot(ld[...], upper, precision=HIGHEST, preferred_element_type=F32)
    for h in range(heads):
        spread = jnp.transpose(jnp.broadcast_to(cum[h : h + 1, :], (LANE, LANE)))
        cc[h] = spread
        d_send[h] = jnp.exp(spread[LANE - 1 : LANE, :])

    k_in.wait()
    v_in.wait()
    for h in range(heads):
        columns = slice(h * LANE, (h + 1) * LANE)
        spread = cc[h]
        tail = jnp.exp(spread[LANE - 1 : LANE, :] - spread)
        faded = (k[:, columns].astype(F32) * tail).astype(BF16)
        state = lax.dot_general(
            faded, v[:, columns], (((0,), (0,)), ((), ())), preferred_element_type=F32
        )
        s_send[h * per_head : (h + 1) * per_head] = state.astype(BF16).reshape(per_head, rows, LANE)

    pl.semaphore_wait(barrier, (group - 1) + (ny - 1) + (nx - 1))

    for r in sorted(range(1, group), key=lambda r: -min(r, group - r)):
        owner = lax.rem(j + r, group)
        for src, dst, sem in (
            (d_send.at[owner // per_head], d_recv, d_sem), (s_send.at[owner], z_recv, z_sem)
        ):
            pltpu.make_async_remote_copy(
                src_ref=src,
                dst_ref=dst.at[j],
                send_sem=sem.at[0],
                recv_sem=sem.at[1],
                device_id={"ctx": base + owner},
                device_id_type=MESH,
            ).start()
    d_recv[pl.ds(j, 1)] = d_send[pl.ds(j // per_head, 1)]
    z_recv[pl.ds(j, 1)] = s_send[pl.ds(j, 1)]

    def weight_copy(r):
        start = pl.multiple_of(lax.rem(x + r, nx) * width, LANE)
        return pltpu.make_async_copy(w_hbm.at[:, pl.ds(start, width)], w.at[r], w_sem.at[0])

    for step in range(half_x):
        distance = half_x - step
        for r in sorted({distance, nx - distance}):
            weight_copy(r).start()
    weight_copy(0).start()

    q_in.wait()
    causal = row_index >= col_index
    for h in range(heads):
        columns = slice(h * LANE, (h + 1) * LANE)
        spread = cc[h]
        scores = lax.dot_general(
            q[:, columns], k[:, columns], (((1,), (1,)), ((), ())), preferred_element_type=F32
        )
        differ = jnp.where(causal, spread - cum[h : h + 1, :], -1e30)
        weights = (jnp.exp(differ) * scores).astype(BF16)
        within[h] = jnp.dot(weights, v[:, columns], preferred_element_type=F32)
        cc[h] = jnp.exp(spread)

    def bulk(ref, send_sem, recv_sem):
        return pltpu.make_async_remote_copy(
            src_ref=ref, dst_ref=ref, send_sem=send_sem, recv_sem=recv_sem,
            device_id={"head": lax.rem(x + 1, nx)}, device_id_type=MESH,
        )

    bulk(d_recv.at[pl.ds(0, group - 1)], d_sem.at[0], d_sem.at[1]).wait_recv()
    running = jnp.ones((1, LANE), F32)
    for i in range(group):
        pd_buf[i] = running
        running = running * d_recv[i]
    yd_send[0] = running

    def row_decay(target):
        return pltpu.make_async_remote_copy(
            src_ref=yd_send.at[0],
            dst_ref=yd_recv.at[y],
            send_sem=yd_send_sem.at[target],
            recv_sem=yd_recv_sem.at[y],
            device_id={"ctx": target * group + j},
            device_id_type=MESH,
        )

    def each_later(act_on):
        for r in offsets:
            @pl.when(y + r < ny)
            def _():
                act_on(y + r)

    each_later(lambda target: row_decay(target).start())

    bulk(z_recv.at[pl.ds(0, group - 1)], z_sem.at[0], z_sem.at[1]).wait_recv()
    carry = jnp.zeros((rows, LANE), F32)
    for i in range(group):
        e_buf[i] = carry
        carry = d_recv[i] * carry + z_recv[i].astype(F32)
    r_send[0] = carry.astype(BF16)

    def row_total(target):
        return pltpu.make_async_remote_copy(
            src_ref=r_send.at[0],
            dst_ref=y_recv.at[y],
            send_sem=y_send_sem.at[target],
            recv_sem=y_recv_sem.at[y],
            device_id={"ctx": target * group + j},
            device_id_type=MESH,
        )

    each_later(lambda target: row_total(target).start())

    def add_row(i, prefix):
        pltpu.make_async_remote_copy(
            src_ref=y_recv.at[i],
            dst_ref=y_recv.at[i],
            send_sem=y_send_sem.at[i],
            recv_sem=y_recv_sem.at[i],
            device_id={"ctx": i * group + j},
            device_id_type=MESH,
        ).wait_recv()
        pltpu.make_async_remote_copy(
            src_ref=yd_recv.at[i],
            dst_ref=yd_recv.at[i],
            send_sem=yd_send_sem.at[i],
            recv_sem=yd_recv_sem.at[i],
            device_id={"ctx": i * group + j},
            device_id_type=MESH,
        ).wait_recv()
        return yd_recv[i] * prefix + y_recv[i].astype(F32)

    prefix = lax.fori_loop(0, y, add_row, jnp.zeros((rows, LANE), F32))

    for i in range(group):
        p_send[i] = (pd_buf[i] * prefix + e_buf[i]).astype(BF16)

        @pl.when(j != i)
        def _():
            pltpu.make_async_remote_copy(
                src_ref=p_send.at[i],
                dst_ref=s_in.at[j],
                send_sem=p_sem.at[0],
                recv_sem=p_sem.at[1],
                device_id={"ctx": base + i},
                device_id_type=MESH,
            ).start()

    s_in[pl.ds(j, 1)] = p_send[pl.ds(j, 1)]

    gain_in.wait()
    pltpu.make_async_copy(w, w, w_sem.at[0]).wait()

    bulk(s_in.at[pl.ds(0, group - 1)], p_sem.at[0], p_sem.at[1]).wait_recv()
    squares = jnp.zeros((LANE, LANE), F32)
    for h in range(heads):
        columns = slice(h * LANE, (h + 1) * LANE)
        state = s_in[h * per_head : (h + 1) * per_head].reshape(LANE, LANE)
        carried = jnp.dot(q[:, columns], state, preferred_element_type=F32)
        attn = within[h] + cc[h] * carried
        squares = squares + attn * attn
        act[:, columns] = (attn * gain[:, columns]).astype(BF16)

    right, left = lax.rem(x + 1, nx), lax.rem(x + nx - 1, nx)

    def slot(step, c, way):
        if step == 0:
            return c if way == 0 else c - half_c
        return half_c + chunks * (step - 1) + c

    def hop(step, c, way):
        place = slot(step, c, way)
        return pltpu.make_async_remote_copy(
            src_ref=tx.at[way, place],
            dst_ref=rx.at[way, place],
            send_sem=tx_sem.at[way],
            recv_sem=rx_sem.at[way, place],
            device_id={"head": right if way == 0 else left},
            device_id_type=MESH,
        )

    def project(r, pair):
        return jnp.dot(
            act[...], w[r, :, pair * 2 * LANE : (pair + 1) * 2 * LANE], preferred_element_type=F32
        )

    for pair in sorted(range(chunks // 2), key=lambda p: min(p, chunks // 2 - 1 - p)):
        block = project(half_x, pair)
        for c in (2 * pair, 2 * pair + 1):
            way = 0 if c < half_c else 1
            part = block[:, :LANE] if c % 2 == 0 else block[:, LANE:]
            tx[way, slot(0, c, way)] = part.astype(BF16)
            hop(0, c, way).start()

    sq_send[0] = jnp.sum(jnp.transpose(squares), axis=0, keepdims=True)

    def send_squares(r, _):
        pltpu.make_async_remote_copy(
            src_ref=sq_send.at[0],
            dst_ref=sq_recv.at[x],
            send_sem=sq_sem.at[0],
            recv_sem=sq_sem.at[1],
            device_id={"head": lax.rem(x + r, nx)},
            device_id_type=MESH,
        ).start()
        return 0

    lax.fori_loop(1, nx, send_squares, 0)
    sq_recv[pl.ds(x, 1)] = sq_send[...]

    def arrives(step, c, way):
        if step == 0:
            return (c < half_c) == (way == 0)
        return True

    def fill(step, way, r):
        for pair in range(chunks // 2):
            block = project(r, pair)
            own[2 * step + way, 2 * pair] = block[:, :LANE]
            own[2 * step + way, 2 * pair + 1] = block[:, LANE:]

    def forward(step, c, way):
        total = own[2 * step + way, c]
        if arrives(step - 1, c, way):
            hop(step - 1, c, way).wait_recv()
            total = total + rx[way, slot(step - 1, c, way)].astype(F32)
        tx[way, slot(step, c, way)] = total.astype(BF16)
        hop(step, c, way).start()

    order = [list(range(half_c, chunks)) + list(range(half_c)), list(range(chunks))]
    for step in range(1, half_x):
        distance = half_x - step
        fill(step, 0, distance)
        fill(step, 1, nx - distance)
        if step == 1:
            for place in range(half_c):
                for way in (0, 1):
                    forward(1, order[way][place], way)
    fill(0, 0, 0)
    for step in range(1, half_x):
        for place in range(half_c if step == 1 else 0, chunks):
            for way in (0, 1):
                forward(step, order[way][place], way)

    bulk(sq_recv.at[pl.ds(0, nx - 1)], sq_sem.at[0], sq_sem.at[1]).wait_recv()
    total = sq_recv[0]
    for i in range(1, nx):
        total = total + sq_recv[i]
    scale = lax.rsqrt(total / (nx * heads * LANE) + 1e-05)
    scale = jnp.transpose(jnp.broadcast_to(scale, (LANE, LANE)))
    for c in range(chunks):
        block = own[0, c]
        for way in (0, 1):
            if arrives(half_x - 1, c, way):
                hop(half_x - 1, c, way).wait_recv()
                block = block + rx[way, slot(half_x - 1, c, way)].astype(F32)
        out_ref[:, c * LANE : (c + 1) * LANE] = (block * scale).astype(BF16)

    bulk(d_recv.at[pl.ds(0, group - 1)], d_sem.at[0], d_sem.at[1]).wait_send()
    bulk(z_recv.at[pl.ds(0, group - 1)], z_sem.at[0], z_sem.at[1]).wait_send()
    bulk(s_in.at[pl.ds(0, group - 1)], p_sem.at[0], p_sem.at[1]).wait_send()
    bulk(sq_recv.at[pl.ds(0, nx - 1)], sq_sem.at[0], sq_sem.at[1]).wait_send()

    def departed(target):
        row_total(target).wait_send()
        row_decay(target).wait_send()

    each_later(departed)
    for way in (0, 1):
        bulk(tx.at[way], tx_sem.at[way], rx_sem.at[way, 0]).wait_send()


def solution(mesh, group=ROW_GROUP):
    nx, ctx = mesh.shape["head"], mesh.shape["ctx"]
    ny = ctx // group

    def local(query, keys, values, log_decay, norm_gain, out_weight):
        tokens, features = query.shape
        heads = log_decay.shape[1]
        width = out_weight.shape[1] // nx
        chunks = width // LANE
        rows = features // group
        slots = chunks // 2 + chunks * (nx // 2 - 1)
        anywhere = pl.BlockSpec(memory_space=pl.ANY)
        square = (LANE, LANE)
        dma = pltpu.SemaphoreType.DMA
        return pl.pallas_call(
            functools.partial(body, (nx, ny, group, heads, chunks)),
            out_shape=pltpu.VMEM((tokens, width), BF16),
            in_specs=[anywhere] * 6,
            out_specs=pl.BlockSpec(memory_space=pltpu.VMEM),
            scratch_shapes=[
                pltpu.VMEM((tokens, features), BF16),
                pltpu.VMEM((tokens, features), BF16),
                pltpu.VMEM((tokens, features), BF16),
                pltpu.VMEM((heads, tokens), F32),
                pltpu.VMEM((1, features), F32),
                pltpu.VMEM((nx, features, width), BF16),
                pltpu.VMEM((heads,) + square, F32),
                pltpu.VMEM((heads,) + square, F32),
                pltpu.VMEM((tokens, features), BF16),
                pltpu.VMEM((heads, 1, LANE), F32),
                pltpu.VMEM((group, 1, LANE), F32),
                pltpu.VMEM((group, rows, LANE), BF16),
                pltpu.VMEM((group, rows, LANE), BF16),
                pltpu.VMEM((group, rows, LANE), F32),
                pltpu.VMEM((group, 1, LANE), F32),
                pltpu.VMEM((1, 1, LANE), F32),
                pltpu.VMEM((ny, 1, LANE), F32),
                pltpu.VMEM((1, rows, LANE), BF16),
                pltpu.VMEM((ny, rows, LANE), BF16),
                pltpu.VMEM((group, rows, LANE), BF16),
                pltpu.VMEM((group, rows, LANE), BF16),
                pltpu.VMEM((1, 1, LANE), F32),
                pltpu.VMEM((nx, 1, LANE), F32),
                pltpu.VMEM((nx, chunks) + square, F32),
                pltpu.VMEM((2, slots) + square, BF16),
                pltpu.VMEM((2, slots) + square, BF16),
                dma((5,)),
                dma((1,)),
                dma((2,)),
                dma((2,)),
                dma((ny,)),
                dma((ny,)),
                dma((ny,)),
                dma((ny,)),
                dma((2,)),
                dma((2,)),
                dma((2,)),
                dma((2, slots)),
            ],
            compiler_params=pltpu.CompilerParams(
                collective_id=0, has_side_effects=True, vmem_limit_bytes=60 * 2**20
            ),
        )(query, keys, values, log_decay.T, norm_gain.reshape(1, features), out_weight)

    placed = (
        P("ctx", "head"),
        P("ctx", "head"),
        P("ctx", "head"),
        P("ctx", "head"),
        P("head"),
        P("head", None),
    )
    return jax.shard_map(
        local, mesh=mesh, in_specs=placed, out_specs=P("ctx", "head"), check_vma=False
    )
```
